32 devices in a mesh: comp: 2 (over x), tile: 16 (over z, y, core).
Axes of the slice: x: 2, y: 2, z: 4, core: 2. Of those that a mesh axis runs over, the one named last changes fastest.
Arguments:
- state: float32 [2, 16, 512, 1024], P('comp', None, 'tile'), may hold values from -6 to 6
- kappa: float32 [2, 16], P('comp'), may hold values from 0.02 to 0.24
- col_mix: float32 [2, 16, 16], P('comp'), may hold values from -1.5 to 1.5
- surface_mask: int32 [2, 512, 1024], P('comp', 'tile'), may hold values 0 or 1
- lagged_flux: float32 [8, 512, 1024], P(None, 'tile'), may hold values from -6 to 6
- a2l_src: int32 [16, 16, 4], P(None, 'tile'), may hold values from 0 to 255
- a2l_dst: int32 [16, 16, 4], P('tile'), may hold values from 0 to 255
- a2l_count: int32 [16, 16], P('tile'), may hold values from 0 to 4, as said below
- a2l_weight: bfloat16 [16, 16, 4, 128, 128], P('tile'), may hold values from 0.049804688 to 1
- l2a_src: int32 [16, 16, 4], P(None, 'tile'), may hold values from 0 to 255
- l2a_dst: int32 [16, 16, 4], P('tile'), may hold values from 0 to 255
- l2a_count: int32 [16, 16], P(None, 'tile'), may hold values from 0 to 4, as said below
- l2a_weight: bfloat16 [16, 16, 4, 128, 128], P(None, 'tile'), may hold values from 0.049804688 to 1
Outputs:
- new_state: float32 [2, 16, 512, 1024], P('comp', None, 'tile')
- fluxes: float32 [2, 8, 512, 1024], P('comp', None, 'tile')
The draws below stay inside these ranges and needn't reach their ends.
Inputs may be any that keep to these rules, and one draw needn't show every extreme that they name: `a2l_count`: for each destination tile, some source tile has exactly 4 live slots. `l2a_count`: for each destination tile, some source tile has exactly 4 live slots.
All inputs are finite; a program needn't handle non-finite values. No bound on the sum of `surface_mask` on one device may be relied on, other than what follows from the above.
Results may differ from the reference program's by a relative error of at most 0.0008.
Values may be sent and summed in bfloat16 or wider, within the bound.
No kernel may reach another device: no remote copies, remote signals or barrier semaphores. Data moves between devices by JAX's collectives and lax.ppermute only.
A program may use at most 128 MiB of HBM per device.

```python
import math
import jax
import jax.numpy as jnp
from jax import lax

LEV = 16
NF = 8
BLK = 128
CAP = 4
NSUB = 2
W = 1024
TILES = 16
NB = 256
NR = 512


def pair_counts(key, salt):
    salted = jax.random.fold_in(key, salt)
    first_key, second_key, third_key = jax.random.split(salted, 3)
    load_level = jax.random.randint(first_key, (TILES, 1), 1, CAP + 1)
    raw_counts = jax.random.randint(second_key, (TILES, TILES), 0, 2 * load_level + 1)
    raw_counts = jnp.minimum(raw_counts, CAP)
    full_pair = jax.random.randint(third_key, (TILES, 1), 0, TILES)
    columns = jnp.arange(TILES, dtype=jnp.int32)[None, :]
    return jnp.where(columns == full_pair, CAP, raw_counts).astype(jnp.int32)


def draw_a2l_count(key, part):
    return pair_counts(key, 7101)


def draw_l2a_count(key, part):
    return pair_counts(key, 7202)


def with_ends(entries, rng, smallest, high):
    index_at = [jax.random.randint(jax.random.fold_in(rng, axis), (), 0, length) for axis, length in enumerate(entries.shape)]
    longest = entries.shape.index(max(entries.shape))
    beside = index_at[:longest] + [(index_at[longest] + 1) % entries.shape[longest]] + index_at[longest + 1:]
    return entries.at[tuple(index_at)].set(smallest).at[tuple(beside)].set(high)


def levels(stream_key, dims, pieces, low, high):
    gain = 1.0
    for position, shards_of in pieces:
        steps = jax.random.uniform(jax.random.fold_in(jax.random.fold_in(stream_key, 6), position), (shards_of,), jnp.float32, low / len(pieces), high / len(pieces))
        gain = gain * jnp.repeat(jnp.exp(steps), dims[position] // shards_of).reshape((-1,) + (1,) * (len(dims) - 1 - position))
    return gain


def normal_values(stream_key, dims, spread, reach, pieces=(), kind=jnp.bfloat16):
    level = levels(stream_key, dims, pieces, -0.22, 0.18) if pieces else 1.0
    entries = jax.random.normal(stream_key, dims, jnp.float32) * spread * level
    return jnp.minimum(jnp.maximum(entries, -reach), reach).astype(kind)


def setup_inputs(seed: int = 0) -> dict:
    seeds = jax.random.split(jax.random.key(seed), 14)
    return {
        "state": normal_values(seeds[0], (2, LEV, NR, W), 1.0, 6.0, ((0, 2), (2, 16)), jnp.float32),
        "kappa": jnp.clip(jnp.exp(math.log(0.24) - 2.4849066 * jax.random.uniform(seeds[1], (2, LEV), jnp.float32) ** levels(seeds[1], (2, LEV), ((0, 2),), -0.2, 0.2)), 0.02, 0.24),
        "col_mix": normal_values(seeds[2], (2, LEV, LEV), LEV ** -0.5, 1.5, ((0, 2),), jnp.float32),
        "surface_mask": with_ends((jax.random.randint(seeds[3], (2, NR, W), 0, 2) < 1).astype(jnp.int32), jax.random.fold_in(seeds[3], 1), 0, 1),
        "lagged_flux": normal_values(seeds[4], (NF, NR, W), 1.0, 6.0, ((1, 16),), jnp.float32),
        "a2l_src": with_ends(jax.random.randint(seeds[5], (TILES, TILES, CAP), 0, NB), jax.random.fold_in(seeds[5], 1), 0, NB - 1).astype(jnp.int32),
        "a2l_dst": with_ends(jax.random.randint(seeds[6], (TILES, TILES, CAP), 0, NB), jax.random.fold_in(seeds[6], 1), 0, NB - 1).astype(jnp.int32),
        "a2l_count": draw_a2l_count(jax.random.fold_in(seeds[13], 71), 0),
        "a2l_weight": jnp.clip(jnp.exp(math.log(1.0) - 2.9996462 * jax.random.uniform(seeds[8], (TILES, TILES, CAP, BLK, BLK), jnp.float32) ** levels(seeds[8], (TILES, TILES, CAP, BLK, BLK), ((0, 16),), -0.2, 0.2)), 0.049804688, 1.0).astype(jnp.bfloat16),
        "l2a_src": with_ends(jax.random.randint(seeds[9], (TILES, TILES, CAP), 0, NB), jax.random.fold_in(seeds[9], 1), 0, NB - 1).astype(jnp.int32),
        "l2a_dst": with_ends(jax.random.randint(seeds[10], (TILES, TILES, CAP), 0, NB), jax.random.fold_in(seeds[10], 1), 0, NB - 1).astype(jnp.int32),
        "l2a_count": draw_l2a_count(jax.random.fold_in(seeds[13], 71), 0),
        "l2a_weight": jnp.clip(jnp.exp(math.log(1.0) - 2.9996462 * jax.random.uniform(seeds[12], (TILES, TILES, CAP, BLK, BLK), jnp.float32) ** levels(seeds[12], (TILES, TILES, CAP, BLK, BLK), ((1, 16),), -0.2, 0.2)), 0.049804688, 1.0).astype(jnp.bfloat16),
    }


def diffuse(fields, rates):
    padded = jnp.pad(fields, ((0, 0), (0, 0), (1, 1), (0, 0)))
    beside_all = padded[:, :, 2:] + padded[:, :, :-2] + jnp.roll(fields, 1, axis=3) + jnp.roll(fields, -1, axis=3)
    return fields + rates * (beside_all - 4.0 * fields)


def block_remap(blocks, index_src, index_dst, counts, weights):
    sources = jnp.arange(TILES, dtype=jnp.int32)[:, None]
    picked = blocks[:, sources, index_src]
    live_slots = (jnp.arange(CAP, dtype=jnp.int32)[None, :] < counts[:, None]).astype(jnp.float32)
    weights_f = weights.astype(jnp.float32)
    contrib = jnp.einsum("fsck,sckm->fscm", picked.astype(jnp.float32), weights_f, precision=lax.Precision.HIGHEST)
    contrib = contrib * live_slots[None, :, :, None]
    column = jnp.sum(weights_f, axis=2) * live_slots[:, :, None]
    onehot = (index_dst.reshape(-1)[:, None] == jnp.arange(NB, dtype=jnp.int32)[None, :]).astype(jnp.float32)
    numerator = jnp.einsum("fem,eb->fbm", contrib.reshape(NF, TILES * CAP, BLK), onehot, precision=lax.Precision.HIGHEST)
    denominator = jnp.einsum("em,eb->bm", column.reshape(TILES * CAP, BLK), onehot, precision=lax.Precision.HIGHEST)
    return numerator / jnp.maximum(denominator, 1.0)[None]


def to_grid(tiled):
    return jnp.transpose(tiled, (1, 0, 2, 3)).reshape(NF, NR, W)


def remap_all(blocks, index_src, index_dst, counts, weights):
    def one_tile(dest_tile):
        return block_remap(blocks, index_src[dest_tile], index_dst[dest_tile], counts[dest_tile], weights[dest_tile])

    return to_grid(lax.map(one_tile, jnp.arange(TILES, dtype=jnp.int32)))


def reference(state, kappa, col_mix, surface_mask, lagged_flux, a2l_src, a2l_dst, a2l_count, a2l_weight, l2a_src, l2a_dst, l2a_count, l2a_weight):
    forcing = state[:, :NF].astype(jnp.bfloat16).reshape(2, NF, TILES, NB, BLK)
    to_land = remap_all(forcing[0], a2l_src, a2l_dst, a2l_count, a2l_weight)
    to_atmos = remap_all(forcing[1], a2l_src, a2l_dst, a2l_count, a2l_weight)
    rates = kappa[:, :, None, None]
    fields = state
    for substep in range(NSUB):
        fields = diffuse(fields, rates)
    incoming = jnp.stack([lagged_flux + to_atmos, to_land])
    land_frac = surface_mask.astype(jnp.float32)[:, None]
    mixing = jnp.einsum("clm,cmrw->clrw", col_mix, fields, precision=lax.Precision.HIGHEST)
    surface = land_frac * incoming - (1.0 - land_frac) * 0.5 * fields[:, :NF]
    new_state = fields + 0.5 * jnp.tanh(mixing)
    new_state = new_state.at[:, :NF].add(surface)
    fluxes_all = land_frac * jnp.tanh(new_state[:, :NF] - incoming)
    flux_sent = fluxes_all.astype(jnp.bfloat16).reshape(2, NF, TILES, NB, BLK)
    atm_flux = remap_all(flux_sent[1], l2a_src, l2a_dst, l2a_count, l2a_weight)
    back_flux = remap_all(flux_sent[0], l2a_src, l2a_dst, l2a_count, l2a_weight)
    return new_state, jnp.stack([atm_flux, fluxes_all[1] + back_flux])
```

```python
import functools

import jax
import jax.numpy as jnp
from jax import lax
from jax.experimental import pallas as pl
from jax.experimental.pallas import tpu as pltpu
from jax.sharding import PartitionSpec as P

NF = 8
BLK = 128
CAP = 4
NSUB = 2
SUB = 8
F32 = jnp.float32
BF16 = jnp.bfloat16
VMEM_LIMIT = 40 * 1024 * 1024


def tile_view(grid):
    levels, rows, cells = grid.shape
    split = grid.reshape(levels, rows // SUB, SUB, cells // BLK, BLK)
    return split.transpose(0, 1, 3, 2, 4).reshape(levels * rows * cells // BLK, BLK)


def from_tile_view(tiles, levels, rows, cells):
    split = tiles.reshape(levels, rows // SUB, cells // BLK, SUB, BLK)
    return split.transpose(0, 1, 3, 2, 4).reshape(levels, rows, cells)


def tile_row(row, x, columns):
    return (lax.div(row, SUB) * columns + x) * SUB + lax.rem(row, SUB)


def block_tile_row(block, columns):
    return tile_row(lax.div(block, columns), lax.rem(block, columns), columns)


def aligned(index, step):
    return pl.multiple_of(index * step, step)


def loop(count, body, unroll=1):
    def step(i, carry):
        body(i)
        return carry

    lax.fori_loop(0, count, step, 0, unroll=unroll)


def pick_kernel(dims, src, state, sent, slab_a, slab_b):
    rows, columns, levels, tiles = dims
    comp, tile = lax.axis_index("comp"), lax.axis_index("tile")
    level_stride = rows * columns
    other = (1 - comp) * tiles

    def one_tile(t):
        for pair in range(CAP // 2):
            two = []
            for k in (2 * pair, 2 * pair + 1):
                start = block_tile_row(src[t, k], columns)
                two.append(state[pl.ds(start, NF, stride=level_stride), :])
            both = jnp.concatenate(two, axis=0).astype(BF16)
            sent[other + t, pl.ds(2 * NF * pair, 2 * NF), :] = both
        sent[comp * tiles + t] = jnp.zeros((CAP * NF, BLK), BF16)

    loop(tiles, one_tile, unroll=4)
    even = lax.rem(tile, 2) == 0
    for slab, first in (
        (slab_a, jnp.where(even, rows - NSUB, 0)),
        (slab_b, jnp.where(even, 0, rows - NSUB)),
    ):
        for i in range(NSUB):
            for x in range(columns):
                start = tile_row(first + i, x, columns)
                value = state[pl.ds(start, levels, stride=level_stride), :]
                slab[(i * columns + x) * levels : (i * columns + x + 1) * levels, :] = value


def prepare_kernel(dims, count, state, lagged, weight, blocks, lagged_blocks, column_sums):
    rows, columns, levels, tiles = dims
    level_stride = rows * columns
    comp = lax.axis_index("comp")
    atmosphere = jnp.where(comp == 0, 1.0, 0.0).astype(F32)

    def one_row(r):
        for x in range(columns):
            start = tile_row(r, x, columns)
            block = r * columns + x
            blocks[pl.ds(aligned(block, levels), levels), :] = state[
                pl.ds(start, levels, stride=level_stride), :
            ]
            lagged_blocks[pl.ds(aligned(block, NF), NF), :] = (
                lagged[pl.ds(start, NF, stride=level_stride), :] * atmosphere
            )

    loop(rows, one_row, unroll=2)
    ones = jnp.ones((2 * SUB, BLK), BF16)

    def one_tile(t):
        live = count[t]
        rows_of = lax.broadcasted_iota(jnp.int32, (SUB, BLK), 0)
        sums = jnp.zeros((SUB, BLK), F32)
        for k in range(CAP):
            column = jnp.dot(ones, weight[t, k], preferred_element_type=F32)[:SUB]
            column = column * jnp.where(k < live, 1.0, 0.0).astype(F32)
            sums = jnp.where((rows_of == k) | (rows_of == k + CAP), column, sums)
        high = sums.astype(BF16).astype(F32)
        column_sums[t] = jnp.where(rows_of < CAP, high, sums - high)

    loop(tiles, one_tile, unroll=4)


def diffuse_kernel(dims, blocks, from_a, from_b, kappa, col_mix, mask, base, deep, stepped):
    rows, columns, levels, tiles = dims
    tile = lax.axis_index("tile")
    even = lax.rem(tile, 2) == 0
    above_in = jnp.where(tile > 0, 1.0, 0.0).astype(F32)
    below_in = jnp.where(tile < tiles - 1, 1.0, 0.0).astype(F32)
    rate = kappa[...]
    keep = 1.0 - 4.0 * rate
    lane = lax.broadcasted_iota(jnp.int32, (levels, BLK), 1)

    def load_row(ref, r):
        return [
            ref[pl.ds(aligned(r * columns + x, levels), levels), :] for x in range(columns)
        ]

    def slab_row(above, i):
        first, second = (from_b, from_a) if above else (from_a, from_b)
        return [
            jnp.where(even, p, q)
            for p, q in zip(load_row(first, i), load_row(second, i), strict=True)
        ]

    def stencil(up, mid, down):
        right_roll = [pltpu.roll(v, 1, 1) for v in mid]
        left_roll = [pltpu.roll(v, BLK - 1, 1) for v in mid]
        out = []
        for x in range(columns):
            west = jnp.where(lane == 0, right_roll[x - 1], right_roll[x])
            east = jnp.where(lane == BLK - 1, left_roll[(x + 1) % columns], left_roll[x])
            out.append(keep * mid[x] + rate * (up[x] + down[x] + (west + east)))
        return out

    def store_stepped(r, values, scale=None):
        for x, v in enumerate(values):
            v = v if scale is None else v * scale
            stepped[pl.ds(aligned((r + 1) * columns + x, levels), levels), :] = v

    above = [slab_row(True, i) for i in range(NSUB)]
    store_stepped(-1, stencil(above[0], above[1], load_row(blocks, 0)), above_in)
    store_stepped(0, stencil(above[1], load_row(blocks, 0), load_row(blocks, 1)))
    below = [slab_row(False, i) for i in range(NSUB)]
    store_stepped(
        rows - 1, stencil(load_row(blocks, rows - 2), load_row(blocks, rows - 1), below[0])
    )
    store_stepped(rows, stencil(load_row(blocks, rows - 1), below[0], below[1]), below_in)

    def first_step(i):
        r = i + 1
        store_stepped(
            r, stencil(load_row(blocks, r - 1), load_row(blocks, r), load_row(blocks, r + 1))
        )

    loop(rows - 2, first_step)
    mix = col_mix[...]
    mix_high = mix.astype(BF16)
    mix_low = (mix - mix_high.astype(F32)).astype(BF16)

    def second_step(r):
        done = stencil(load_row(stepped, r), load_row(stepped, r + 1), load_row(stepped, r + 2))
        whole = jnp.concatenate(done, axis=1)
        high = whole.astype(BF16)
        low = (whole - high.astype(F32)).astype(BF16)
        mixed = (
            jnp.dot(mix_high, high, preferred_element_type=F32)
            + jnp.dot(mix_high, low, preferred_element_type=F32)
            + jnp.dot(mix_low, high, preferred_element_type=F32)
        )
        moved = whole + 0.5 * jnp.tanh(mixed)
        land = mask[0, pl.ds(r, 1), :].astype(F32)
        top = moved[:NF] - (0.5 * (1.0 - land)) * whole[:NF]
        rest = moved[NF:]
        for x in range(columns):
            where = r * columns + x
            cells = slice(x * BLK, (x + 1) * BLK)
            base[pl.ds(aligned(where, NF), NF), :] = top[:, cells]
            deep[pl.ds(aligned(where, levels - NF), levels - NF), :] = rest[:, cells]

    loop(rows, second_step)


def surface_kernel(
    dims, dst, live_in, src, live_out, arrived, weight_in, base, lagged, mask, weight_out, column_sums,
    sent, top, flux, numerator, denominator,
):
    rows, columns, _, tiles = dims
    comp = lax.axis_index("comp")
    other = (1 - comp) * tiles

    def clear(r):
        for x in range(columns):
            where = pl.ds(aligned(r * columns + x, NF), NF)
            numerator[where, :] = jnp.zeros((NF, BLK), F32)
            denominator[where, :] = jnp.zeros((NF, BLK), F32)

    loop(rows, clear, unroll=4)
    ones = jnp.ones((NF, BLK), F32)

    def receive(t):
        got = arrived[other + t].astype(F32)
        for k in range(CAP):
            both = jnp.concatenate([got[k * NF : (k + 1) * NF], ones], axis=0).astype(BF16)
            product = jnp.dot(both, weight_in[t, k], preferred_element_type=F32)
            live = jnp.where(k < live_in[t], 1.0, 0.0).astype(F32)
            product = product * live
            where = pl.ds(aligned(dst[t, k], NF), NF)
            numerator[where, :] += product[:NF]
            denominator[where, :] += product[NF:]

    loop(tiles, receive, unroll=4)

    def one_row(r):
        land_row = mask[0, pl.ds(r, 1), :].astype(F32)
        for x in range(columns):
            where = pl.ds(aligned(r * columns + x, NF), NF)
            land = land_row[:, x * BLK : (x + 1) * BLK]
            received = numerator[where, :] / jnp.maximum(denominator[where, :], 1.0)
            incoming = lagged[where, :] + received
            state = base[where, :] + land * incoming
            top[where, :] = state
            flux[where, :] = land * jnp.tanh(state - incoming)

    loop(rows, one_row)

    def send(t):
        for pair in range(CAP // 2):
            two = []
            for k in (2 * pair, 2 * pair + 1):
                picked = flux[pl.ds(aligned(src[t, k], NF), NF), :].astype(BF16)
                product = jnp.dot(picked, weight_out[t, k], preferred_element_type=F32)
                two.append(product * jnp.where(k < live_out[t], 1.0, 0.0).astype(F32))
            both = jnp.concatenate(two, axis=0).astype(BF16)
            sent[other + t, pl.ds(2 * NF * pair, 2 * NF), :] = both
        sums = jnp.concatenate([column_sums[t], jnp.zeros((SUB, BLK), F32)], axis=0)
        sent[comp * tiles + t, pl.ds(0, 2 * SUB), :] = sums.astype(BF16)
        sent[comp * tiles + t, pl.ds(2 * SUB, 2 * SUB), :] = jnp.zeros((2 * SUB, BLK), BF16)

    loop(tiles, send, unroll=4)


def write_kernel(dims, top, deep, flux, new_state, land_flux):
    rows, columns, levels, _ = dims
    comp = lax.axis_index("comp")
    on_land = jnp.where(comp == 1, 1.0, 0.0).astype(F32)
    depth = levels - NF

    def one(rt):
        for x in range(columns):
            for level in range(NF):
                out = pl.ds(aligned((level * (rows // SUB) + rt) * columns + x, SUB), SUB)
                start = (rt * SUB * columns + x) * NF + level
                new_state[out, :] = top[pl.ds(start, SUB, stride=columns * NF), :]
                land_flux[out, :] = flux[pl.ds(start, SUB, stride=columns * NF), :] * on_land
            for level in range(depth):
                out = pl.ds(aligned(((level + NF) * (rows // SUB) + rt) * columns + x, SUB), SUB)
                start = (rt * SUB * columns + x) * depth + level
                new_state[out, :] = deep[pl.ds(start, SUB, stride=columns * depth), :]

    loop(rows // SUB, one)


def return_kernel(dims, dst, arrived, land_flux, fluxes, numerator, denominator):
    rows, columns, _, tiles = dims
    comp = lax.axis_index("comp")
    other = (1 - comp) * tiles
    level_stride = rows * columns

    def clear(t):
        for k in range(CAP):
            where = pl.ds(aligned(dst[t, k], NF), NF)
            numerator[where, :] = jnp.zeros((NF, BLK), F32)
            denominator[where, :] = jnp.zeros((NF, BLK), F32)

    loop(tiles, clear, unroll=4)

    def copy(i):
        where = pl.ds(aligned(i, columns * SUB), columns * SUB)
        fluxes[where, :] = land_flux[where, :]

    loop(NF * rows // SUB, copy, unroll=4)

    def receive(t):
        got = arrived[other + t].astype(F32)
        sums = arrived[comp * tiles + t].astype(F32)
        sums = sums[:CAP] + sums[CAP : 2 * CAP]
        for k in range(CAP):
            where = pl.ds(aligned(dst[t, k], NF), NF)
            numerator[where, :] += got[k * NF : (k + 1) * NF]
            denominator[where, :] += jnp.broadcast_to(sums[k : k + 1], (NF, BLK))

    loop(tiles, receive, unroll=4)

    def finish(t):
        for k in range(CAP):
            block = dst[t, k]
            where = pl.ds(aligned(block, NF), NF)
            out = pl.ds(block_tile_row(block, columns), NF, stride=level_stride)
            value = numerator[where, :] / jnp.maximum(denominator[where, :], 1.0)
            fluxes[out, :] = land_flux[out, :] + value

    loop(tiles, finish, unroll=4)


def call(kernel, scalars, arrays, outs, scratch=(), cost=0):
    smem = pl.BlockSpec(memory_space=pltpu.SMEM)
    vmem = pl.BlockSpec(memory_space=pltpu.VMEM)
    return pl.pallas_call(
        kernel,
        out_shape=outs,
        in_specs=[smem] * len(scalars) + [vmem] * len(arrays),
        out_specs=tuple([vmem] * len(outs)),
        scratch_shapes=list(scratch),
        compiler_params=pltpu.CompilerParams(vmem_limit_bytes=VMEM_LIMIT),
        cost_estimate=pl.CostEstimate(flops=cost, bytes_accessed=cost // 4, transcendentals=0),
    )(*scalars, *arrays)


def per_device(
    state,
    kappa,
    col_mix,
    surface_mask,
    lagged_flux,
    a2l_src,
    a2l_dst,
    a2l_count,
    a2l_weight,
    l2a_src,
    l2a_dst,
    l2a_count,
    l2a_weight,
):
    fields = state[0]
    levels, rows, cells = fields.shape
    columns = cells // BLK
    nblocks = rows * columns
    tiles = lax.axis_size("tile")
    dims = (rows, columns, levels, tiles)
    shape = jax.ShapeDtypeStruct
    kernel = lambda f: functools.partial(f, dims)
    state_tiles = tile_view(fields)
    slab = shape((NSUB * columns * levels, BLK), F32)
    parcel = shape((2 * tiles, CAP * NF, BLK), BF16)
    sent, slab_a, slab_b = call(
        kernel(pick_kernel), [a2l_src[:, 0, :]], [state_tiles], [parcel, slab, slab],
        cost=4_000_000,
    )
    arrived = lax.all_to_all(sent, ("comp", "tile"), split_axis=0, concat_axis=0, tiled=True)
    from_a = lax.ppermute(slab_a, "tile", [(i, i ^ 1) for i in range(tiles)])
    pairs = [(i, i + 1) for i in range(1, tiles - 1, 2)]
    from_b = lax.ppermute(slab_b, "tile", pairs + [(j, i) for i, j in pairs])
    blocks, lagged_blocks, column_sums = call(
        kernel(prepare_kernel), [l2a_count[:, 0]],
        [state_tiles, tile_view(lagged_flux), l2a_weight[:, 0]],
        [pltpu.VMEM((nblocks * levels, BLK), F32), pltpu.VMEM((nblocks * NF, BLK), F32),
         pltpu.VMEM((tiles, SUB, BLK), F32)],
        cost=20_000_000,
    )
    base, deep = call(
        kernel(diffuse_kernel), [],
        [blocks, from_a, from_b, jnp.broadcast_to(kappa[0][:, None], (levels, BLK)), col_mix[0],
         surface_mask],
        [pltpu.VMEM((nblocks * NF, BLK), F32), pltpu.VMEM((nblocks * (levels - NF), BLK), F32)],
        scratch=[pltpu.VMEM(((rows + 2) * columns * levels, BLK), F32)],
        cost=40_000_000,
    )
    sent_back, top, flux = call(
        kernel(surface_kernel), [a2l_dst[0], a2l_count[0], l2a_src[:, 0, :], l2a_count[:, 0]],
        [arrived, a2l_weight[0], base, lagged_blocks, surface_mask, l2a_weight[:, 0], column_sums],
        [parcel, pltpu.VMEM((nblocks * NF, BLK), F32), pltpu.VMEM((nblocks * NF, BLK), F32)],
        scratch=[pltpu.VMEM((nblocks * NF, BLK), F32), pltpu.VMEM((nblocks * NF, BLK), F32)],
        cost=20_000_000,
    )
    returned = lax.all_to_all(sent_back, ("comp", "tile"), split_axis=0, concat_axis=0, tiled=True)
    new_state, land_flux = call(
        kernel(write_kernel), [], [top, deep, flux],
        [shape((levels * nblocks, BLK), F32), pltpu.VMEM((NF * nblocks, BLK), F32)],
        cost=20_000_000,
    )
    (fluxes,) = call(
        kernel(return_kernel), [l2a_dst[0]], [returned, land_flux],
        [shape((NF * nblocks, BLK), F32)],
        scratch=[pltpu.VMEM((nblocks * NF, BLK), F32), pltpu.VMEM((nblocks * NF, BLK), F32)],
        cost=10_000_000,
    )
    return (
        from_tile_view(new_state, levels, rows, cells)[None],
        from_tile_view(fluxes, NF, rows, cells)[None],
    )


def solution(mesh):
    return jax.shard_map(
        per_device,
        mesh=mesh,
        in_specs=(
            P("comp", None, "tile", None),
            P("comp", None),
            P("comp", None, None),
            P("comp", "tile", None),
            P(None, "tile", None),
            P(None, "tile", None),
            P("tile", None, None),
            P("tile", None),
            P("tile", None, None, None, None),
            P(None, "tile", None),
            P("tile", None, None),
            P(None, "tile"),
            P(None, "tile", None, None, None),
        ),
        out_specs=(P("comp", None, "tile", None), P("comp", None, "tile", None)),
        check_vma=False,
    )
```

```python
import functools

import jax
import jax.numpy as jnp
from jax import lax
from jax.experimental import pallas as pl
from jax.experimental.pallas import tpu as pltpu
from jax.sharding import PartitionSpec as P

NF = 8
BLK = 128
CAP = 4
NSUB = 2
SUB = 8
F32 = jnp.float32
BF16 = jnp.bfloat16
VMEM_LIMIT = 12 * 1024 * 1024


def tile_view(grid):
    levels, rows, cells = grid.shape
    split = grid.reshape(levels, rows // SUB, SUB, cells // BLK, BLK)
    return split.transpose(0, 1, 3, 2, 4).reshape(levels * rows * cells // BLK, BLK)


def from_tile_view(tiles, levels, rows, cells):
    split = tiles.reshape(levels, rows // SUB, cells // BLK, SUB, BLK)
    return split.transpose(0, 1, 3, 2, 4).reshape(levels, rows, cells)


def tile_row(row, x, columns):
    return (lax.div(row, SUB) * columns + x) * SUB + lax.rem(row, SUB)


def block_tile_row(block, columns):
    return tile_row(lax.div(block, columns), lax.rem(block, columns), columns)


def aligned(index, step):
    return pl.multiple_of(index * step, step)


def loop(count, body, unroll=1):
    def step(i, carry):
        body(i)
        return carry

    lax.fori_loop(0, count, step, 0, unroll=min(unroll, count))


class Copies:
    def __init__(self, semaphores):
        self.semaphores, self.open, self.used = semaphores, {}, 0

    def start(self, name, source, target):
        copy = pltpu.make_async_copy(source, target, self.semaphores.at[self.used])
        self.used += 1
        copy.start()
        self.open[name] = copy

    def wait(self, *names):
        for name in names:
            self.open.pop(name).wait()

    def wait_all(self):
        self.wait(*list(self.open))


def parts_of(count, parts):
    parts = parts if count % parts == 0 else 1
    return [pl.ds(i * (count // parts), count // parts) for i in range(parts)]


def pick_kernel(dims, src_in, state_in, sent_out, slab_a_out, slab_b_out, src, state, sent, slab_a, slab_b, sems):
    rows, columns, levels, tiles = dims
    copies = Copies(sems)
    level_stride = rows * columns
    copies.start("src", src_in, src)
    for i, part in enumerate(parts_of(NF * level_stride, 4)):
        copies.start(("top", i), state_in.at[part], state.at[part])
    deep = pl.ds(NF * level_stride, (levels - NF) * level_stride)
    copies.start("deep", state_in.at[deep], state.at[deep])
    comp, tile = lax.axis_index("comp"), lax.axis_index("tile")
    other = (1 - comp) * tiles

    def blank(t):
        sent[comp * tiles + t] = jnp.zeros((CAP * NF, BLK), BF16)

    loop(tiles, blank, unroll=16)

    def one_tile(t):
        for pair in range(CAP // 2):
            two = []
            for k in (2 * pair, 2 * pair + 1):
                start = block_tile_row(src[k, t], columns)
                two.append(state[pl.ds(start, NF, stride=level_stride), :])
            both = jnp.concatenate(two, axis=0).astype(BF16)
            sent[other + t, pl.ds(2 * NF * pair, 2 * NF), :] = both

    copies.wait("src", *[("top", i) for i in range(len(parts_of(NF * level_stride, 4)))])
    loop(tiles, one_tile, unroll=16)
    for name, half in (("sent", other), ("own", comp * tiles)):
        where = pl.ds(half, tiles)
        copies.start(name, sent.at[where], sent_out.at[where])
    even = lax.rem(tile, 2) == 0
    copies.wait("deep")
    for slab, first in (
        (slab_a, jnp.where(even, rows - NSUB, 0)),
        (slab_b, jnp.where(even, 0, rows - NSUB)),
    ):
        for i in range(NSUB):
            for x in range(columns):
                start = tile_row(first + i, x, columns)
                value = state[pl.ds(start, levels, stride=level_stride), :]
                slab[(i * columns + x) * levels : (i * columns + x + 1) * levels, :] = value
    copies.start("a", slab_a, slab_a_out)
    copies.start("b", slab_b, slab_b_out)
    copies.wait_all()


def prepare_kernel(
    dims, count_in, state_in, lagged_in, weight_in, blocks, lagged_out, sums_out,
    count, state, lagged, weight, lagged_blocks, column_sums, sems,
):
    rows, columns, levels, tiles = dims
    copies = Copies(sems)
    level_stride = rows * columns
    for i, part in enumerate(parts_of(levels * level_stride, 4)):
        copies.start(("state", i), state_in.at[part], state.at[part])
    copies.start("count", count_in, count)
    for i, part in enumerate(parts_of(NF * level_stride, 2)):
        copies.start(("lagged", i), lagged_in.at[part], lagged.at[part])
    for i, part in enumerate(parts_of(tiles, 4)):
        copies.start(("weight", i), weight_in.at[part], weight.at[part])
    comp = lax.axis_index("comp")
    atmosphere = jnp.where(comp == 0, 1.0, 0.0).astype(F32)

    def one_row(r):
        for x in range(columns):
            start = tile_row(r, x, columns)
            block = r * columns + x
            blocks[pl.ds(aligned(block, levels), levels), :] = state[
                pl.ds(start, levels, stride=level_stride), :
            ]

    def lagged_row(r):
        for x in range(columns):
            start = tile_row(r, x, columns)
            lagged_blocks[pl.ds(aligned(r * columns + x, NF), NF), :] = (
                lagged[pl.ds(start, NF, stride=level_stride), :] * atmosphere
            )

    copies.wait(*[("state", i) for i in range(len(parts_of(levels * level_stride, 4)))])
    loop(rows, one_row, unroll=32)
    copies.wait(*[("lagged", i) for i in range(len(parts_of(NF * level_stride, 2)))])
    loop(rows, lagged_row, unroll=32)
    copies.start("lagged_blocks", lagged_blocks, lagged_out)
    ones = jnp.ones((2 * SUB, BLK), BF16)
    rows_of = lax.broadcasted_iota(jnp.int32, (SUB, BLK), 0)
    copies.wait("count")

    def one_tile(t):
        live = count[t]
        sums = jnp.zeros((SUB, BLK), F32)
        for k in range(CAP):
            column = jnp.dot(ones, weight[t, k], preferred_element_type=F32)[:SUB]
            column = column * jnp.where(k < live, 1.0, 0.0).astype(F32)
            sums = jnp.where((rows_of == k) | (rows_of == k + CAP), column, sums)
        high = sums.astype(BF16).astype(F32)
        column_sums[t] = jnp.where(rows_of < CAP, high, sums - high)

    for i, part in enumerate(parts_of(tiles, 4)):
        copies.wait(("weight", i))
        loop(part.size, lambda t, part=part: one_tile(part.start + t), unroll=16)
    copies.start("sums", column_sums, sums_out)
    copies.wait_all()


def diffuse_kernel(
    dims, blocks, kappa, col_mix, from_a_in, from_b_in, mask_in, base_out, deep_out,
    from_a, from_b, mask, base, deep, stepped, sems,
):
    rows, columns, levels, tiles = dims
    copies = Copies(sems)
    copies.start("a", from_a_in, from_a)
    copies.start("b", from_b_in, from_b)
    copies.start("mask", mask_in, mask)
    tile = lax.axis_index("tile")
    even = lax.rem(tile, 2) == 0
    above_in = jnp.where(tile > 0, 1.0, 0.0).astype(F32)
    below_in = jnp.where(tile < tiles - 1, 1.0, 0.0).astype(F32)
    rate = kappa[...]
    keep = 1.0 - 4.0 * rate
    lane = lax.broadcasted_iota(jnp.int32, (levels, BLK), 1)

    def load_row(ref, r):
        return [
            ref[pl.ds(aligned(r * columns + x, levels), levels), :] for x in range(columns)
        ]

    def slab_row(above, i):
        first, second = (from_b, from_a) if above else (from_a, from_b)
        return [
            jnp.where(even, p, q)
            for p, q in zip(load_row(first, i), load_row(second, i), strict=True)
        ]

    def stencil(up, mid, down):
        right_roll = [pltpu.roll(v, 1, 1) for v in mid]
        left_roll = [pltpu.roll(v, BLK - 1, 1) for v in mid]
        out = []
        for x in range(columns):
            west = jnp.where(lane == 0, right_roll[x - 1], right_roll[x])
            east = jnp.where(lane == BLK - 1, left_roll[(x + 1) % columns], left_roll[x])
            out.append(keep * mid[x] + rate * (up[x] + down[x] + (west + east)))
        return out

    def store_stepped(r, values, scale=None):
        for x, v in enumerate(values):
            v = v if scale is None else v * scale
            stepped[pl.ds(aligned((r + 1) * columns + x, levels), levels), :] = v

    def first_step(i):
        r = i + 1
        store_stepped(
            r, stencil(load_row(blocks, r - 1), load_row(blocks, r), load_row(blocks, r + 1))
        )

    loop(rows - 2, first_step, unroll=30)
    copies.wait("a", "b")
    above = [slab_row(True, i) for i in range(NSUB)]
    store_stepped(-1, stencil(above[0], above[1], load_row(blocks, 0)), above_in)
    store_stepped(0, stencil(above[1], load_row(blocks, 0), load_row(blocks, 1)))
    below = [slab_row(False, i) for i in range(NSUB)]
    store_stepped(
        rows - 1, stencil(load_row(blocks, rows - 2), load_row(blocks, rows - 1), below[0])
    )
    store_stepped(rows, stencil(load_row(blocks, rows - 1), below[0], below[1]), below_in)
    mix = col_mix[...]
    mix_high = mix.astype(BF16)
    mix_low = (mix - mix_high.astype(F32)).astype(BF16)
    mix_three = jnp.concatenate([mix_high, mix_high, mix_low], axis=1)
    copies.wait("mask")

    def second_step(r):
        done = stencil(load_row(stepped, r), load_row(stepped, r + 1), load_row(stepped, r + 2))
        whole = jnp.concatenate(done, axis=1)
        high = whole.astype(BF16)
        low = (whole - high.astype(F32)).astype(BF16)
        three = jnp.concatenate([high, low, high], axis=0)
        mixed = jnp.dot(mix_three, three, preferred_element_type=F32)
        moved = whole + 0.5 * jnp.tanh(mixed)
        land = mask[0, pl.ds(r, 1), :].astype(F32)
        top = moved[:NF] - (0.5 * (1.0 - land)) * whole[:NF]
        rest = moved[NF:]
        for x in range(columns):
            where = r * columns + x
            cells = slice(x * BLK, (x + 1) * BLK)
            base[pl.ds(aligned(where, NF), NF), :] = top[:, cells]
            deep[pl.ds(aligned(where, levels - NF), levels - NF), :] = rest[:, cells]

    for i, part in enumerate(parts_of(rows, 2)):
        loop(part.size, lambda r, part=part: second_step(part.start + r), unroll=16)
        for name, source, target, depth in (
            ("base", base, base_out, NF), ("deep", deep, deep_out, levels - NF),
        ):
            where = pl.ds(part.start * columns * depth, part.size * columns * depth)
            copies.start((name, i), source.at[where], target.at[where])
    copies.wait_all()


def surface_kernel(
    dims, arrived, dst_in, live_in_in, src_in, live_out_in, weight_in_in, base_in, lagged_in, mask_in, weight_out_in,
    sums_in, sent_out, top_out, flux_out,
    dst, live_in, src, live_out, weight_in, base, lagged, mask, weight_out, column_sums, sent, top, flux,
    numerator, denominator, sems,
):
    rows, columns, _, tiles = dims
    copies = Copies(sems)
    copies.start("dst", dst_in, dst)
    copies.start("live_in", live_in_in, live_in)
    tile_parts = parts_of(tiles, 4)
    for i, part in enumerate(tile_parts):
        copies.start(("weight_in", i), weight_in_in.at[part], weight_in.at[part])
    copies.start("base", base_in, base)
    copies.start("lagged", lagged_in, lagged)
    copies.start("mask", mask_in, mask)
    copies.start("src", src_in, src)
    copies.start("live_out", live_out_in, live_out)
    copies.start("sums", sums_in, column_sums)
    for i, part in enumerate(tile_parts):
        copies.start(("weight_out", i), weight_out_in.at[part], weight_out.at[part])
    comp = lax.axis_index("comp")
    other, own = (1 - comp) * tiles, comp * tiles

    def clear(r):
        for x in range(columns):
            where = pl.ds(aligned(r * columns + x, NF), NF)
            numerator[where, :] = jnp.zeros((NF, BLK), F32)
            denominator[where, :] = jnp.zeros((NF, BLK), F32)

    loop(rows, clear, unroll=32)
    ones = jnp.ones((NF, BLK), F32)

    def receive(t):
        got = arrived[other + t].astype(F32)
        for k in range(CAP):
            both = jnp.concatenate([got[k * NF : (k + 1) * NF], ones], axis=0).astype(BF16)
            product = jnp.dot(both, weight_in[t, k], preferred_element_type=F32)
            live = jnp.where(k < live_in[t], 1.0, 0.0).astype(F32)
            product = product * live
            where = pl.ds(aligned(dst[k, t], NF), NF)
            numerator[where, :] += product[:NF]
            denominator[where, :] += product[NF:]

    copies.wait("dst", "live_in")
    for i, part in enumerate(tile_parts):
        copies.wait(("weight_in", i))
        loop(part.size, lambda t, part=part: receive(part.start + t), unroll=16)
    copies.wait("base", "lagged", "mask")

    def one_row(r):
        land_row = mask[0, pl.ds(r, 1), :].astype(F32)
        for x in range(columns):
            where = pl.ds(aligned(r * columns + x, NF), NF)
            land = land_row[:, x * BLK : (x + 1) * BLK]
            received = numerator[where, :] / jnp.maximum(denominator[where, :], 1.0)
            incoming = lagged[where, :] + received
            state = base[where, :] + land * incoming
            top[where, :] = state
            flux[where, :] = land * jnp.tanh(state - incoming)

    loop(rows, one_row, unroll=32)
    copies.start("top", top, top_out)
    copies.start("flux", flux, flux_out)

    def send(t):
        for pair in range(CAP // 2):
            two = []
            for k in (2 * pair, 2 * pair + 1):
                picked = flux[pl.ds(aligned(src[k, t], NF), NF), :].astype(BF16)
                product = jnp.dot(picked, weight_out[t, k], preferred_element_type=F32)
                two.append(product * jnp.where(k < live_out[t], 1.0, 0.0).astype(F32))
            both = jnp.concatenate(two, axis=0).astype(BF16)
            sent[other + t, pl.ds(2 * NF * pair, 2 * NF), :] = both
        sums = jnp.concatenate([column_sums[t], jnp.zeros((SUB, BLK), F32)], axis=0)
        sent[own + t, pl.ds(0, 2 * SUB), :] = sums.astype(BF16)
        sent[own + t, pl.ds(2 * SUB, 2 * SUB), :] = jnp.zeros((2 * SUB, BLK), BF16)

    copies.wait("src", "live_out", "sums")
    for i, part in enumerate(tile_parts):
        copies.wait(("weight_out", i))
        loop(part.size, lambda t, part=part: send(part.start + t), unroll=16)
        for half in (other, own):
            where = pl.ds(half + part.start, part.size)
            copies.start(("sent", i, half is own), sent.at[where], sent_out.at[where])
    copies.wait_all()


def write_kernel(dims, top_in, deep_in, flux_in, new_state_out, land_flux_out, top, deep, flux, new_state, land_flux, sems):
    rows, columns, levels, _ = dims
    copies = Copies(sems)
    copies.start("top", top_in, top)
    copies.start("deep", deep_in, deep)
    copies.start("flux", flux_in, flux)
    comp = lax.axis_index("comp")
    on_land = jnp.where(comp == 1, 1.0, 0.0).astype(F32)
    depth = levels - NF
    cut = NF * rows * columns

    def from_blocks(source, target, count, first, scale=None):
        def one(rt):
            for x in range(columns):
                for level in range(count):
                    out = ((level + first) * (rows // SUB) + rt) * columns + x
                    start = (rt * SUB * columns + x) * count + level
                    value = source[pl.ds(start, SUB, stride=columns * count), :]
                    value = value if scale is None else value * scale
                    target[pl.ds(aligned(out, SUB), SUB), :] = value

        loop(rows // SUB, one, unroll=4)

    copies.wait("top")
    from_blocks(top, new_state, NF, 0)
    copies.start("state", new_state.at[pl.ds(0, cut)], new_state_out.at[pl.ds(0, cut)])
    copies.wait("deep")
    from_blocks(deep, new_state, depth, NF)
    rest = pl.ds(cut, depth * rows * columns)
    copies.start("rest", new_state.at[rest], new_state_out.at[rest])
    copies.wait("flux")
    from_blocks(flux, land_flux, NF, 0, on_land)
    copies.start("land", land_flux, land_flux_out)
    copies.wait_all()


def return_kernel(dims, arrived, dst_in, land_flux_in, fluxes_out, dst, land_flux, fluxes, numerator, denominator, sems):
    rows, columns, _, tiles = dims
    copies = Copies(sems)
    copies.start("dst", dst_in, dst)
    halves = parts_of(NF * rows * columns, 2)
    for i, part in enumerate(halves):
        copies.start(("land", i), land_flux_in.at[part], land_flux.at[part])
        copies.start(("fluxes", i), land_flux_in.at[part], fluxes.at[part])
    comp = lax.axis_index("comp")
    other = (1 - comp) * tiles
    level_stride = rows * columns

    def clear(r):
        for x in range(columns):
            where = pl.ds(aligned(r * columns + x, NF), NF)
            numerator[where, :] = jnp.zeros((NF, BLK), F32)
            denominator[where, :] = jnp.zeros((NF, BLK), F32)

    loop(rows, clear, unroll=32)

    def receive(t):
        got = arrived[other + t].astype(F32)
        sums = arrived[comp * tiles + t].astype(F32)
        sums = sums[:CAP] + sums[CAP : 2 * CAP]
        for k in range(CAP):
            where = pl.ds(aligned(dst[k, t], NF), NF)
            numerator[where, :] += got[k * NF : (k + 1) * NF]
            denominator[where, :] += jnp.broadcast_to(sums[k : k + 1], (NF, BLK))

    copies.wait("dst")
    loop(tiles, receive, unroll=16)
    copies.wait_all()

    def finish(t):
        for k in range(CAP):
            block = dst[k, t]
            where = pl.ds(aligned(block, NF), NF)
            out = pl.ds(block_tile_row(block, columns), NF, stride=level_stride)
            value = numerator[where, :] / jnp.maximum(denominator[where, :], 1.0)
            fluxes[out, :] = land_flux[out, :] + value

    loop(tiles, finish, unroll=16)
    for i, part in enumerate(halves):
        copies.start(("out", i), fluxes.at[part], fluxes_out.at[part])
    copies.wait_all()


def call(kernel, operands, places, outs, scratch, copies, limit, cost):
    spec = {"v": pl.BlockSpec(memory_space=pltpu.VMEM), "h": pl.BlockSpec(memory_space=pltpu.HBM)}
    operands = [
        pltpu.with_memory_space_constraint(x, pltpu.HBM) if place == "h" else x
        for x, place in zip(operands, places, strict=True)
    ]
    return pl.pallas_call(
        kernel,
        out_shape=[out for out, _ in outs],
        in_specs=[spec[place] for place in places],
        out_specs=[spec[place] for _, place in outs],
        scratch_shapes=[*scratch, pltpu.SemaphoreType.DMA((copies,))],
        compiler_params=pltpu.CompilerParams(vmem_limit_bytes=limit),
        cost_estimate=pl.CostEstimate(flops=cost, bytes_accessed=cost // 4, transcendentals=0),
    )(*operands)


def per_device(
    state,
    kappa,
    col_mix,
    surface_mask,
    lagged_flux,
    a2l_src,
    a2l_dst,
    a2l_count,
    a2l_weight,
    l2a_src,
    l2a_dst,
    l2a_count,
    l2a_weight,
):
    fields = state[0]
    levels, rows, cells = fields.shape
    columns = cells // BLK
    nblocks = rows * columns
    tiles = lax.axis_size("tile")
    dims = (rows, columns, levels, tiles)
    shape, vmem, smem = pltpu.HBM, pltpu.VMEM, pltpu.SMEM
    kernel = lambda f: functools.partial(f, dims)
    limit = VMEM_LIMIT + 4 * tiles * CAP * BLK * BLK
    state_tiles = tile_view(fields)
    slab = (NSUB * columns * levels, BLK)
    parcel = (2 * tiles, CAP * NF, BLK)
    top_shape = (nblocks * NF, BLK)
    deep_shape = (nblocks * (levels - NF), BLK)
    full_shape = (nblocks * levels, BLK)
    sums_shape = (tiles, SUB, BLK)
    weight_shape = (tiles, CAP, BLK, BLK)
    slots, counts = smem((CAP, tiles), jnp.int32), smem((tiles,), jnp.int32)
    sent, slab_a, slab_b = call(
        kernel(pick_kernel), [a2l_src[:, 0, :].T, state_tiles], "hh",
        [(shape(parcel, BF16), "h"), (shape(slab, F32), "h"), (shape(slab, F32), "h")],
        [slots, vmem(full_shape, F32), vmem(parcel, BF16), vmem(slab, F32), vmem(slab, F32)],
        10, limit, 4_000_000,
    )
    arrived = lax.all_to_all(sent, ("comp", "tile"), split_axis=0, concat_axis=0, tiled=True)
    from_a = lax.ppermute(slab_a, "tile", [(i, i ^ 1) for i in range(tiles)])
    pairs = [(i, i + 1) for i in range(1, tiles - 1, 2)]
    from_b = lax.ppermute(slab_b, "tile", pairs + [(j, i) for i, j in pairs])
    blocks, lagged_blocks, column_sums = call(
        kernel(prepare_kernel),
        [l2a_count[:, 0], state_tiles, tile_view(lagged_flux), l2a_weight[:, 0]], "hhhh",
        [(vmem(full_shape, F32), "v"), (shape(top_shape, F32), "h"), (shape(sums_shape, F32), "h")],
        [counts, vmem(full_shape, F32), vmem(top_shape, F32), vmem(weight_shape, BF16),
         vmem(top_shape, F32), vmem(sums_shape, F32)],
        13, limit, 20_000_000,
    )
    base, deep = call(
        kernel(diffuse_kernel),
        [blocks, jnp.broadcast_to(kappa[0][:, None], (levels, BLK)), col_mix[0], from_a, from_b,
         surface_mask], "vvvhhh",
        [(shape(top_shape, F32), "h"), (shape(deep_shape, F32), "h")],
        [vmem(slab, F32), vmem(slab, F32), vmem((1, rows, cells), jnp.int32), vmem(top_shape, F32),
         vmem(deep_shape, F32), vmem(((rows + 2) * columns * levels, BLK), F32)],
        7, limit, 20_000_000,
    )
    sent_back, top, flux = call(
        kernel(surface_kernel),
        [arrived, a2l_dst[0].T, a2l_count[0], l2a_src[:, 0, :].T, l2a_count[:, 0], a2l_weight[0], base,
         lagged_blocks, surface_mask, l2a_weight[:, 0], column_sums], "vhhhhhhhhhh",
        [(shape(parcel, BF16), "h"), (shape(top_shape, F32), "h"), (shape(top_shape, F32), "h")],
        [slots, counts, slots, counts, vmem(weight_shape, BF16), vmem(top_shape, F32),
         vmem(top_shape, F32), vmem((1, rows, cells), jnp.int32), vmem(weight_shape, BF16),
         vmem(sums_shape, F32), vmem(parcel, BF16), vmem(top_shape, F32), vmem(top_shape, F32),
         vmem(top_shape, F32), vmem(top_shape, F32)],
        26, limit, 20_000_000,
    )
    returned = lax.all_to_all(
        sent_back, ("comp", "tile"), split_axis=0, concat_axis=0, tiled=True
    )
    new_state, land_flux = call(
        kernel(write_kernel), [top, deep, flux], "hhh",
        [(shape(full_shape, F32), "h"), (shape(top_shape, F32), "h")],
        [vmem(top_shape, F32), vmem(deep_shape, F32), vmem(top_shape, F32), vmem(full_shape, F32),
         vmem(top_shape, F32)],
        6, limit, 20_000_000,
    )
    (fluxes,) = call(
        kernel(return_kernel), [returned, l2a_dst[0].T, land_flux], "vhh",
        [(shape(top_shape, F32), "h")],
        [slots, vmem(top_shape, F32), vmem(top_shape, F32), vmem(top_shape, F32), vmem(top_shape, F32)],
        7, limit, 10_000_000,
    )
    return (
        from_tile_view(new_state, levels, rows, cells)[None],
        from_tile_view(fluxes, NF, rows, cells)[None],
    )


def solution(mesh):
    return jax.shard_map(
        per_device,
        mesh=mesh,
        in_specs=(
            P("comp", None, "tile", None),
            P("comp", None),
            P("comp", None, None),
            P("comp", "tile", None),
            P(None, "tile", None),
            P(None, "tile", None),
            P("tile", None, None),
            P("tile", None),
            P("tile", None, None, None, None),
            P(None, "tile", None),
            P("tile", None, None),
            P(None, "tile"),
            P(None, "tile", None, None, None),
        ),
        out_specs=(P("comp", None, "tile", None), P("comp", None, "tile", None)),
        check_vma=False,
    )
```

```python
import functools

import jax
import jax.numpy as jnp
from jax import lax
from jax.experimental import pallas as pl
from jax.experimental.pallas import tpu as pltpu
from jax.sharding import PartitionSpec as P


NF = 8
BLK = 128
CAP = 4
NSUB = 2
SUB = 8
F32 = jnp.float32
BF16 = jnp.bfloat16
VMEM_LIMIT = 12 * 1024 * 1024


def tile_view(grid):
    levels, rows, cells = grid.shape
    split = grid.reshape(levels, rows // SUB, SUB, cells // BLK, BLK)
    return split.transpose(0, 1, 3, 2, 4).reshape(levels * rows * cells // BLK, BLK)


def from_tile_view(tiles, levels, rows, cells):
    split = tiles.reshape(levels, rows // SUB, cells // BLK, SUB, BLK)
    return split.transpose(0, 1, 3, 2, 4).reshape(levels, rows, cells)


def tile_row(row, x, columns):
    return (lax.div(row, SUB) * columns + x) * SUB + lax.rem(row, SUB)


def block_tile_row(block, columns):
    return tile_row(lax.div(block, columns), lax.rem(block, columns), columns)


def aligned(index, step):
    return pl.multiple_of(index * step, step)


def loop(count, body, unroll=1):
    def step(i, carry):
        body(i)
        return carry

    lax.fori_loop(0, count, step, 0, unroll=min(unroll, count))


class Copies:
    def __init__(self, semaphores):
        self.semaphores, self.open, self.used = semaphores, {}, 0

    def start(self, name, source, target):
        copy = pltpu.make_async_copy(source, target, self.semaphores.at[self.used])
        self.used += 1
        copy.start()
        self.open[name] = copy

    def wait(self, *names):
        for name in names:
            self.open.pop(name).wait()

    def wait_all(self):
        self.wait(*list(self.open))


def parts_of(count, parts):
    parts = parts if count % parts == 0 else 1
    return [pl.ds(i * (count // parts), count // parts) for i in range(parts)]


def pick_kernel(dims, src_in, state_in, sent_out, slab_a, slab_b, src, state, sent, sems):
    rows, columns, levels, tiles = dims
    copies = Copies(sems)
    level_stride = rows * columns
    copies.start("src", src_in, src)
    for i, part in enumerate(parts_of(NF * level_stride, 4)):
        copies.start(("top", i), state_in.at[part], state.at[part])
    deep = pl.ds(NF * level_stride, (levels - NF) * level_stride)
    copies.start("deep", state_in.at[deep], state.at[deep])
    comp, tile = lax.axis_index("comp"), lax.axis_index("tile")
    other = (1 - comp) * tiles

    def blank(t):
        sent[comp * tiles + t] = jnp.zeros((CAP * NF, BLK), BF16)

    loop(tiles, blank, unroll=16)

    def one_tile(t):
        for pair in range(CAP // 2):
            two = []
            for k in (2 * pair, 2 * pair + 1):
                start = block_tile_row(src[k, t], columns)
                two.append(state[pl.ds(start, NF, stride=level_stride), :])
            both = jnp.concatenate(two, axis=0).astype(BF16)
            sent[other + t, pl.ds(2 * NF * pair, 2 * NF), :] = both

    copies.wait("src", *[("top", i) for i in range(len(parts_of(NF * level_stride, 4)))])
    loop(tiles, one_tile, unroll=16)
    for name, half in (("sent", other), ("own", comp * tiles)):
        where = pl.ds(half, tiles)
        copies.start(name, sent.at[where], sent_out.at[where])
    even = lax.rem(tile, 2) == 0
    copies.wait("deep")
    for slab, first in (
        (slab_a, jnp.where(even, rows - NSUB, 0)),
        (slab_b, jnp.where(even, 0, rows - NSUB)),
    ):
        for i in range(NSUB):
            for x in range(columns):
                start = tile_row(first + i, x, columns)
                value = state[pl.ds(start, levels, stride=level_stride), :]
                slab[(i * columns + x) * levels : (i * columns + x + 1) * levels, :] = value.astype(BF16)
    copies.wait_all()


def row_of(ref, r, columns, levels):
    return [ref[pl.ds(aligned(r * columns + x, levels), levels), :] for x in range(columns)]


def put_row(ref, r, values, columns, levels):
    for x, v in enumerate(values):
        ref[pl.ds(aligned(r * columns + x, levels), levels), :] = v


def stencil(rate, up, mid, down):
    columns = len(mid)
    keep = 1.0 - 4.0 * rate
    lane = lax.broadcasted_iota(jnp.int32, rate.shape, 1)
    right_roll = [pltpu.roll(v, 1, 1) for v in mid]
    left_roll = [pltpu.roll(v, BLK - 1, 1) for v in mid]
    out = []
    for x in range(columns):
        west = jnp.where(lane == 0, right_roll[x - 1], right_roll[x])
        east = jnp.where(lane == BLK - 1, left_roll[(x + 1) % columns], left_roll[x])
        out.append(keep * mid[x] + rate * (up[x] + down[x] + (west + east)))
    return out


def mixing_of(col_mix):
    mix_high = col_mix.astype(BF16)
    mix_low = (col_mix - mix_high.astype(F32)).astype(BF16)
    return jnp.concatenate([mix_high, mix_high, mix_low], axis=1)


def column_physics(diffused, mixing, land):
    whole = jnp.concatenate(diffused, axis=1)
    high = whole.astype(BF16)
    low = (whole - high.astype(F32)).astype(BF16)
    three = jnp.concatenate([high, low, high], axis=0)
    moved = whole + 0.5 * jnp.tanh(jnp.dot(mixing, three, preferred_element_type=F32))
    top = moved[:NF] - (0.5 * (1.0 - land)) * whole[:NF]
    columns = len(diffused)
    cut = lambda v: [v[:, x * BLK : (x + 1) * BLK] for x in range(columns)]
    return cut(top), cut(moved[NF:])


def inner_kernel(
    dims, kappa, state_in, mask_in, mix_in, weight_in, near, base_out, deep_out, mask_edge, mix, weight,
    mask, state, blocks, stepped, base, deep, sems,
):
    rows, columns, levels, _ = dims
    depth = levels - NF
    copies = Copies(sems)
    level_stride = rows * columns
    parts = parts_of(rows // SUB, 4)
    for i, part in enumerate(parts):
        where = pl.ds(part.start * columns * SUB, part.size * columns * SUB)
        copies.start(i, state_in.at[:, where], state.at[:, where])
    copies.start("mask", mask_in, mask)
    copies.start("mix", mix_in, mix)
    copies.start("weight", weight_in, weight)
    flat = state.reshape(levels * level_stride, BLK)
    rate = kappa[...]

    def one_row(r):
        put_row(
            blocks, r,
            [flat[pl.ds(tile_row(r, x, columns), levels, stride=level_stride), :] for x in range(columns)],
            columns, levels,
        )

    def first_step(r):
        around = [row_of(blocks, r + i, columns, levels) for i in (-1, 0, 1)]
        put_row(stepped, r, stencil(rate, *around), columns, levels)

    done = 1
    for i, part in enumerate(parts):
        copies.wait(i)
        first, size = part.start * SUB, part.size * SUB
        loop(size, lambda r, first=first: one_row(first + r), unroll=size)
        last = first + size - 1
        loop(last - done, lambda r, done=done: first_step(done + r), unroll=last - done)
        done = last
    for i, r in enumerate((0, 1, rows - 2, rows - 1)):
        put_row(near, i, row_of(blocks, r, columns, levels), columns, levels)
    for i, r in enumerate((1, 2, rows - 3, rows - 2)):
        put_row(near, 4 + i, row_of(stepped, r, columns, levels), columns, levels)
    copies.wait("mask", "mix")
    for i, r in enumerate((0, 1, rows - 2, rows - 1)):
        mask_edge[i : i + 1, :] = mask[0, r : r + 1, :]
    mixing = mixing_of(mix[...])

    def second_step(i):
        r = i + 2
        around = [row_of(stepped, r + j, columns, levels) for j in (-1, 0, 1)]
        land = mask[0, pl.ds(r, 1), :].astype(F32)
        top, rest = column_physics(stencil(rate, *around), mixing, land)
        put_row(base, r, top, columns, NF)
        put_row(deep, r, rest, columns, depth)

    loop(rows - 4, second_step, unroll=28)
    for name, source, target, size in (("base", base, base_out, NF), ("deep", deep, deep_out, depth)):
        middle = pl.ds(2 * columns * size, (rows - 4) * columns * size)
        copies.start(name, source.at[middle], target.at[middle])
    copies.wait_all()


def edge_kernel(dims, kappa, near, mask_edge, mix, from_a, from_b, base_edge, deep, stepped, sems):
    _, columns, levels, tiles = dims
    tile = lax.axis_index("tile")
    even = lax.rem(tile, 2) == 0
    above_in = jnp.where(tile > 0, 1.0, 0.0).astype(F32)
    below_in = jnp.where(tile < tiles - 1, 1.0, 0.0).astype(F32)
    rate = kappa[...]
    mixing = mixing_of(mix[...])

    def slab_row(above, i):
        first, second = (from_b, from_a) if above else (from_a, from_b)
        return [
            jnp.where(even, p.astype(F32), q.astype(F32))
            for p, q in zip(
                row_of(first, i, columns, levels), row_of(second, i, columns, levels), strict=True
            )
        ]

    old = [row_of(near, i, columns, levels) for i in range(4)]
    above = [slab_row(True, i) for i in range(NSUB)]
    below = [slab_row(False, i) for i in range(NSUB)]
    new = [
        [v * above_in for v in stencil(rate, above[0], above[1], old[0])],
        stencil(rate, above[1], old[0], old[1]),
        stencil(rate, old[2], old[3], below[0]),
        [v * below_in for v in stencil(rate, old[3], below[0], below[1])],
    ]
    for i, values in enumerate(new):
        put_row(stepped, i, values, columns, levels)
    new = lambda i: row_of(stepped, i, columns, levels)
    at = lambda i: row_of(near, 4 + i, columns, levels)
    for i, around in enumerate(
        (
            (new(0), new(1), at(0)),
            (new(1), at(0), at(1)),
            (at(2), at(3), new(2)),
            (at(3), new(2), new(3)),
        )
    ):
        land = mask_edge[i : i + 1, :].astype(F32)
        top, rest = column_physics(stencil(rate, *around), mixing, land)
        put_row(base_edge, i, top, columns, NF)
        put_row(deep, i, rest, columns, levels - NF)


def surface_kernel(
    dims, arrived, base_edge, deep_edge, weight_in, dst_in, live_in_in, src_in, live_out_in, base_in, lagged_in, mask_in, weight_out_in,
    sent_out, top_out, flux_out, deep_edge_out,
    dst, live_in, src, live_out, base, lagged, mask, weight_out, sent, top, flux,
    numerator, denominator, sems,
):
    rows, columns, _, tiles = dims
    copies = Copies(sems)
    copies.start("dst", dst_in, dst)
    copies.start("live_in", live_in_in, live_in)
    tile_parts = parts_of(tiles, 4)
    middle = pl.ds(2 * columns * NF, (rows - 4) * columns * NF)
    copies.start("base", base_in.at[middle], base.at[middle])
    copies.start("lagged", lagged_in, lagged)
    copies.start("mask", mask_in, mask)
    copies.start("src", src_in, src)
    copies.start("live_out", live_out_in, live_out)
    for i, part in enumerate(tile_parts):
        copies.start(("weight_out", i), weight_out_in.at[part], weight_out.at[part])
    copies.start("deep_edge", deep_edge, deep_edge_out)
    comp = lax.axis_index("comp")
    other, own = (1 - comp) * tiles, comp * tiles

    def clear(r):
        for x in range(columns):
            where = pl.ds(aligned(r * columns + x, NF), NF)
            numerator[where, :] = jnp.zeros((NF, BLK), F32)
            denominator[where, :] = jnp.zeros((NF, BLK), F32)

    loop(rows, clear, unroll=32)
    ones = jnp.ones((NF, BLK), F32)

    def receive(t):
        got = arrived[other + t].astype(F32)
        for k in range(CAP):
            both = jnp.concatenate([got[k * NF : (k + 1) * NF], ones], axis=0).astype(BF16)
            product = jnp.dot(both, weight_in[t, k], preferred_element_type=F32)
            live = jnp.where(k < live_in[t], 1.0, 0.0).astype(F32)
            product = product * live
            where = pl.ds(aligned(dst[k, t], NF), NF)
            numerator[where, :] += product[:NF]
            denominator[where, :] += product[NF:]

    copies.wait("dst", "live_in")
    loop(tiles, receive, unroll=16)
    copies.wait("base", "lagged", "mask")
    atmosphere = jnp.where(comp == 0, 1.0, 0.0).astype(F32)

    def one_row(r, held=base, held_row=None):
        held_row = r if held_row is None else held_row
        land_row = mask[0, pl.ds(r, 1), :].astype(F32)
        for x in range(columns):
            where = pl.ds(aligned(r * columns + x, NF), NF)
            land = land_row[:, x * BLK : (x + 1) * BLK]
            received = numerator[where, :] / jnp.maximum(denominator[where, :], 1.0)
            before = lagged[pl.ds(tile_row(r, x, columns), NF, stride=rows * columns), :]
            incoming = before * atmosphere + received
            state = held[pl.ds(aligned(held_row * columns + x, NF), NF), :] + land * incoming
            top[where, :] = state
            flux[where, :] = land * jnp.tanh(state - incoming)

    loop(rows - 4, lambda i: one_row(i + 2), unroll=28)
    for i, r in enumerate((0, 1, rows - 2, rows - 1)):
        one_row(r, base_edge, i)
    copies.start("top", top, top_out)
    copies.start("flux", flux, flux_out)

    rows_of = lax.broadcasted_iota(jnp.int32, (SUB, BLK), 0)

    def send(t):
        sums = jnp.zeros((SUB, BLK), F32)
        for pair in range(CAP // 2):
            two = []
            for k in (2 * pair, 2 * pair + 1):
                picked = flux[pl.ds(aligned(src[k, t], NF), NF), :]
                both = jnp.concatenate([picked, ones], axis=0).astype(BF16)
                product = jnp.dot(both, weight_out[t, k], preferred_element_type=F32)
                product = product * jnp.where(k < live_out[t], 1.0, 0.0).astype(F32)
                two.append(product[:NF])
                sums = jnp.where((rows_of == k) | (rows_of == k + CAP), product[NF:], sums)
            both = jnp.concatenate(two, axis=0).astype(BF16)
            sent[other + t, pl.ds(2 * NF * pair, 2 * NF), :] = both
        high = sums.astype(BF16).astype(F32)
        sums = jnp.where(rows_of < CAP, high, sums - high)
        sums = jnp.concatenate([sums, jnp.zeros((SUB, BLK), F32)], axis=0)
        sent[own + t, pl.ds(0, 2 * SUB), :] = sums.astype(BF16)
        sent[own + t, pl.ds(2 * SUB, 2 * SUB), :] = jnp.zeros((2 * SUB, BLK), BF16)

    copies.wait("src", "live_out")
    for i, part in enumerate(tile_parts):
        copies.wait(("weight_out", i))
        loop(part.size, lambda t, part=part: send(part.start + t), unroll=16)
        for half in (other, own):
            where = pl.ds(half + part.start, part.size)
            copies.start(("sent", i, half is own), sent.at[where], sent_out.at[where])
    copies.wait_all()


def write_kernel(dims, top_in, deep_in, deep_edge_in, flux_in, new_state_out, land_flux, top, deep, flux, new_state, sems):
    rows, columns, levels, _ = dims
    copies = Copies(sems)
    copies.start("top", top_in, top)
    depth = levels - NF
    row, two = columns * depth, 2 * columns * depth
    for name, source, first, target, size in (
        ("deep", deep_in, two, two, (rows - 4) * row),
        ("above", deep_edge_in, 0, 0, two),
        ("below", deep_edge_in, two, (rows - 2) * row, two),
    ):
        copies.start(name, source.at[pl.ds(first, size)], deep.at[pl.ds(target, size)])
    copies.start("flux", flux_in, flux)
    comp = lax.axis_index("comp")
    on_land = jnp.where(comp == 1, 1.0, 0.0).astype(F32)
    cut = NF * rows * columns

    def from_blocks(source, target, count, first, scale=None):
        def one(rt):
            for x in range(columns):
                for level in range(count):
                    out = ((level + first) * (rows // SUB) + rt) * columns + x
                    start = (rt * SUB * columns + x) * count + level
                    value = source[pl.ds(start, SUB, stride=columns * count), :]
                    value = value if scale is None else value * scale
                    target[pl.ds(aligned(out, SUB), SUB), :] = value

        loop(rows // SUB, one, unroll=4)

    copies.wait("top")
    from_blocks(top, new_state, NF, 0)
    copies.start("state", new_state.at[pl.ds(0, cut)], new_state_out.at[pl.ds(0, cut)])
    copies.wait("deep", "above", "below")
    from_blocks(deep, new_state, depth, NF)
    rest = pl.ds(cut, depth * rows * columns)
    copies.start("rest", new_state.at[rest], new_state_out.at[rest])
    copies.wait("flux")
    from_blocks(flux, land_flux, NF, 0, on_land)
    copies.wait_all()


def return_kernel(dims, arrived, land_flux, dst_in, fluxes_out, dst, fluxes, numerator, denominator, sems):
    rows, columns, _, tiles = dims
    copies = Copies(sems)
    copies.start("dst", dst_in, dst)
    halves = parts_of(NF * rows * columns, 2)
    for i, part in enumerate(halves):
        copies.start(i, land_flux.at[part], fluxes.at[part])
    comp = lax.axis_index("comp")
    other = (1 - comp) * tiles
    level_stride = rows * columns

    def clear(r):
        for x in range(columns):
            where = pl.ds(aligned(r * columns + x, NF), NF)
            numerator[where, :] = jnp.zeros((NF, BLK), F32)
            denominator[where, :] = jnp.zeros((NF, BLK), F32)

    loop(rows, clear, unroll=32)

    def receive(t):
        got = arrived[other + t].astype(F32)
        sums = arrived[comp * tiles + t].astype(F32)
        sums = sums[:CAP] + sums[CAP : 2 * CAP]
        for k in range(CAP):
            where = pl.ds(aligned(dst[k, t], NF), NF)
            numerator[where, :] += got[k * NF : (k + 1) * NF]
            denominator[where, :] += jnp.broadcast_to(sums[k : k + 1], (NF, BLK))

    copies.wait("dst")
    loop(tiles, receive, unroll=16)
    copies.wait_all()

    def finish(t):
        for k in range(CAP):
            block = dst[k, t]
            where = pl.ds(aligned(block, NF), NF)
            out = pl.ds(block_tile_row(block, columns), NF, stride=level_stride)
            value = numerator[where, :] / jnp.maximum(denominator[where, :], 1.0)
            fluxes[out, :] = land_flux[out, :] + value

    loop(tiles, finish, unroll=16)
    for i, part in enumerate(halves):
        copies.start(("out", i), fluxes.at[part], fluxes_out.at[part])
    copies.wait_all()


def call(kernel, operands, places, outs, scratch, copies, limit, cost):
    vmem, hbm = pl.BlockSpec(memory_space=pltpu.VMEM), pl.BlockSpec(memory_space=pltpu.HBM)
    spec = {"v": vmem, "m": vmem, "h": hbm}
    space = {"m": pltpu.VMEM, "h": pltpu.HBM}
    operands = [
        pltpu.with_memory_space_constraint(x, space[place]) if place in space else x
        for x, place in zip(operands, places, strict=True)
    ]
    return pl.pallas_call(
        kernel,
        out_shape=[out for out, _ in outs],
        in_specs=[spec[place] for place in places],
        out_specs=[spec[place] for _, place in outs],
        scratch_shapes=[*scratch, pltpu.SemaphoreType.DMA((copies,))],
        compiler_params=pltpu.CompilerParams(vmem_limit_bytes=limit),
        cost_estimate=pl.CostEstimate(flops=cost, bytes_accessed=cost // 4, transcendentals=0),
    )(*operands)


def per_device(
    state,
    kappa,
    col_mix,
    surface_mask,
    lagged_flux,
    a2l_src,
    a2l_dst,
    a2l_count,
    a2l_weight,
    l2a_src,
    l2a_dst,
    l2a_count,
    l2a_weight,
):
    fields = state[0]
    levels, rows, cells = fields.shape
    columns = cells // BLK
    nblocks = rows * columns
    tiles = lax.axis_size("tile")
    dims = (rows, columns, levels, tiles)
    shape, vmem, smem = pltpu.HBM, pltpu.VMEM, pltpu.SMEM
    kernel = lambda f: functools.partial(f, dims)
    limit = VMEM_LIMIT + 4 * tiles * CAP * BLK * BLK
    state_tiles = tile_view(fields)
    slab = (NSUB * columns * levels, BLK)
    parcel = (2 * tiles, CAP * NF, BLK)
    top_shape = (nblocks * NF, BLK)
    deep_shape = (nblocks * (levels - NF), BLK)
    full_shape = (nblocks * levels, BLK)
    weight_shape = (tiles, CAP, BLK, BLK)
    slots, counts = smem((CAP, tiles), jnp.int32), smem((tiles,), jnp.int32)
    sent, slab_a, slab_b = call(
        kernel(pick_kernel), [a2l_src[:, 0, :].T, state_tiles], "hh",
        [(shape(parcel, BF16), "h"), (vmem(slab, BF16), "v"), (vmem(slab, BF16), "v")],
        [slots, vmem(full_shape, F32), vmem(parcel, BF16)],
        8, limit, 4_000_000,
    )
    arrived = lax.all_to_all(sent, ("comp", "tile"), split_axis=0, concat_axis=0, tiled=True)
    from_a = lax.ppermute(slab_a, "tile", [(i, i ^ 1) for i in range(tiles)])
    pairs = [(i, i + 1) for i in range(1, tiles - 1, 2)]
    from_b = lax.ppermute(slab_b, "tile", pairs + [(j, i) for i, j in pairs])
    rates = jnp.broadcast_to(kappa[0][:, None], (levels, BLK))
    near, base, deep, mask_edge, mix, weight_in = call(
        kernel(inner_kernel),
        [rates, state_tiles.reshape(levels, nblocks, BLK), surface_mask, col_mix[0], a2l_weight[0]], "vhhhh",
        [(vmem((8 * columns * levels, BLK), F32), "v"), (shape(top_shape, F32), "h"),
         (shape(deep_shape, F32), "h"), (vmem((4, cells), jnp.int32), "v"),
         (vmem((levels, levels), F32), "v"), (vmem(weight_shape, BF16), "v")],
        [vmem((1, rows, cells), jnp.int32), vmem((levels, nblocks, BLK), F32), vmem(full_shape, F32),
         vmem(full_shape, F32), vmem(top_shape, F32), vmem(deep_shape, F32)],
        9, limit, 20_000_000,
    )
    base_edge, deep_near = call(
        kernel(edge_kernel), [rates, near, mask_edge, mix, from_a, from_b], "vvvvvv",
        [(vmem((4 * columns * NF, BLK), F32), "v"), (vmem((4 * columns * (levels - NF), BLK), F32), "v")],
        [vmem((4 * columns * levels, BLK), F32)],
        1, limit, 4_000_000,
    )
    sent_back, top, flux, deep_edge = call(
        kernel(surface_kernel),
        [arrived, base_edge, deep_near, weight_in, a2l_dst[0].T, a2l_count[0], l2a_src[:, 0, :].T,
         l2a_count[:, 0], base, tile_view(lagged_flux), surface_mask, l2a_weight[:, 0]], "vvvvhhhhhhhh",
        [(shape(parcel, BF16), "h"), (shape(top_shape, F32), "h"), (shape(top_shape, F32), "h"),
         (shape((4 * columns * (levels - NF), BLK), F32), "h")],
        [slots, counts, slots, counts, vmem(top_shape, F32), vmem(top_shape, F32), vmem((1, rows, cells), jnp.int32),
         vmem(weight_shape, BF16), vmem(parcel, BF16), vmem(top_shape, F32), vmem(top_shape, F32), vmem(top_shape, F32), vmem(top_shape, F32)],
        23, limit, 20_000_000,
    )
    returned = lax.all_to_all(
        sent_back, ("comp", "tile"), split_axis=0, concat_axis=0, tiled=True
    )
    new_state, land_flux = call(
        kernel(write_kernel), [top, deep, deep_edge, flux], "hhhh",
        [(shape(full_shape, F32), "h"), (vmem(top_shape, F32), "v")],
        [vmem(top_shape, F32), vmem(deep_shape, F32), vmem(top_shape, F32), vmem(full_shape, F32),
         ],
        8, limit, 20_000_000,
    )
    (fluxes,) = call(
        kernel(return_kernel), [returned, land_flux, l2a_dst[0].T], "vvh",
        [(shape(top_shape, F32), "h")],
        [slots, vmem(top_shape, F32), vmem(top_shape, F32), vmem(top_shape, F32)],
        6, limit, 10_000_000,
    )
    return (
        from_tile_view(new_state, levels, rows, cells)[None],
        from_tile_view(fluxes, NF, rows, cells)[None],
    )


def solution(mesh):
    return jax.shard_map(
        per_device,
        mesh=mesh,
        in_specs=(
            P("comp", None, "tile", None),
            P("comp", None),
            P("comp", None, None),
            P("comp", "tile", None),
            P(None, "tile", None),
            P(None, "tile", None),
            P("tile", None, None),
            P("tile", None),
            P("tile", None, None, None, None),
            P(None, "tile", None),
            P("tile", None, None),
            P(None, "tile"),
            P(None, "tile", None, None, None),
        ),
        out_specs=(P("comp", None, "tile", None), P("comp", None, "tile", None)),
        check_vma=False,
    )
```

```python
import functools

import jax
import jax.numpy as jnp
from jax import lax
from jax.experimental import pallas as pl
from jax.experimental.pallas import tpu as pltpu
from jax.sharding import PartitionSpec as P


NF = 8
BLK = 128
CAP = 4
NSUB = 2
SUB = 8
F32 = jnp.float32
BF16 = jnp.bfloat16
VMEM_LIMIT = 12 * 1024 * 1024


def tile_view(grid):
    levels, rows, cells = grid.shape
    split = grid.reshape(levels, rows // SUB, SUB, cells // BLK, BLK)
    return split.transpose(0, 1, 3, 2, 4).reshape(levels * rows * cells // BLK, BLK)


def from_tile_view(tiles, levels, rows, cells):
    split = tiles.reshape(levels, rows // SUB, cells // BLK, SUB, BLK)
    return split.transpose(0, 1, 3, 2, 4).reshape(levels, rows, cells)


def tile_row(row, x, columns):
    return (lax.div(row, SUB) * columns + x) * SUB + lax.rem(row, SUB)


def block_tile_row(block, columns):
    return tile_row(lax.div(block, columns), lax.rem(block, columns), columns)


def aligned(index, step):
    return pl.multiple_of(index * step, step)


def loop(count, body, unroll=1):
    def step(i, carry):
        body(i)
        return carry

    lax.fori_loop(0, count, step, 0, unroll=min(unroll, count))


class Copies:
    def __init__(self, semaphores):
        self.semaphores, self.open, self.used = semaphores, {}, 0

    def start(self, name, source, target):
        copy = pltpu.make_async_copy(source, target, self.semaphores.at[self.used])
        self.used += 1
        copy.start()
        self.open[name] = copy

    def wait(self, *names):
        for name in names:
            self.open.pop(name).wait()

    def wait_all(self):
        self.wait(*list(self.open))


def parts_of(count, parts):
    parts = parts if count % parts == 0 else 1
    return [pl.ds(i * (count // parts), count // parts) for i in range(parts)]


def pick_kernel(dims, src_in, state_in, sent_out, slab_a, slab_b, src, state, sent, sems):
    rows, columns, levels, tiles = dims
    copies = Copies(sems)
    level_stride = rows * columns
    copies.start("src", src_in, src)
    for i, part in enumerate(parts_of(NF * level_stride, 4)):
        copies.start(("top", i), state_in.at[part], state.at[part])
    deep = pl.ds(NF * level_stride, (levels - NF) * level_stride)
    copies.start("deep", state_in.at[deep], state.at[deep])
    comp, tile = lax.axis_index("comp"), lax.axis_index("tile")
    other = (1 - comp) * tiles

    def blank(t):
        sent[comp * tiles + t] = jnp.zeros((CAP * NF, BLK), BF16)

    loop(tiles, blank, unroll=16)

    def one_tile(t):
        for pair in range(CAP // 2):
            two = []
            for k in (2 * pair, 2 * pair + 1):
                start = block_tile_row(src[k, t], columns)
                two.append(state[pl.ds(start, NF, stride=level_stride), :])
            both = jnp.concatenate(two, axis=0).astype(BF16)
            sent[other + t, pl.ds(2 * NF * pair, 2 * NF), :] = both

    copies.wait("src", *[("top", i) for i in range(len(parts_of(NF * level_stride, 4)))])
    loop(tiles, one_tile, unroll=16)
    for name, half in (("sent", other), ("own", comp * tiles)):
        where = pl.ds(half, tiles)
        copies.start(name, sent.at[where], sent_out.at[where])
    even = lax.rem(tile, 2) == 0
    copies.wait("deep")
    for slab, first in (
        (slab_a, jnp.where(even, rows - NSUB, 0)),
        (slab_b, jnp.where(even, 0, rows - NSUB)),
    ):
        for i in range(NSUB):
            for x in range(columns):
                start = tile_row(first + i, x, columns)
                value = state[pl.ds(start, levels, stride=level_stride), :]
                slab[(i * columns + x) * levels : (i * columns + x + 1) * levels, :] = value.astype(BF16)
    copies.wait_all()


def row_of(ref, r, columns, levels):
    return [ref[pl.ds(aligned(r * columns + x, levels), levels), :] for x in range(columns)]


def put_row(ref, r, values, columns, levels):
    for x, v in enumerate(values):
        ref[pl.ds(aligned(r * columns + x, levels), levels), :] = v


def stencil(rate, up, mid, down):
    columns = len(mid)
    keep = 1.0 - 4.0 * rate
    lane = lax.broadcasted_iota(jnp.int32, rate.shape, 1)
    right_roll = [pltpu.roll(v, 1, 1) for v in mid]
    left_roll = [pltpu.roll(v, BLK - 1, 1) for v in mid]
    out = []
    for x in range(columns):
        west = jnp.where(lane == 0, right_roll[x - 1], right_roll[x])
        east = jnp.where(lane == BLK - 1, left_roll[(x + 1) % columns], left_roll[x])
        out.append(keep * mid[x] + rate * (up[x] + down[x] + (west + east)))
    return out


def mixing_of(col_mix):
    mix_high = col_mix.astype(BF16)
    mix_low = (col_mix - mix_high.astype(F32)).astype(BF16)
    return jnp.concatenate([mix_high, mix_high, mix_low], axis=1)


def column_physics(diffused, mixing, land):
    whole = jnp.concatenate(diffused, axis=1)
    high = whole.astype(BF16)
    low = (whole - high.astype(F32)).astype(BF16)
    three = jnp.concatenate([high, low, high], axis=0)
    moved = whole + 0.5 * jnp.tanh(jnp.dot(mixing, three, preferred_element_type=F32))
    top = moved[:NF] - (0.5 * (1.0 - land)) * whole[:NF]
    columns = len(diffused)
    cut = lambda v: [v[:, x * BLK : (x + 1) * BLK] for x in range(columns)]
    return cut(top), cut(moved[NF:])


def inner_kernel(
    dims, kappa, state_in, mask_in, mix_in, weight_in, near, base_out, deep_out, mask_edge, mix, weight,
    mask, state, blocks, stepped, base, deep, sems,
):
    rows, columns, levels, _ = dims
    depth = levels - NF
    copies = Copies(sems)
    level_stride = rows * columns
    parts = parts_of(rows // SUB, 4)
    for i, part in enumerate(parts):
        where = pl.ds(part.start * columns * SUB, part.size * columns * SUB)
        copies.start(i, state_in.at[:, where], state.at[:, where])
    copies.start("mask", mask_in, mask)
    copies.start("mix", mix_in, mix)
    copies.start("weight", weight_in, weight)
    flat = state.reshape(levels * level_stride, BLK)
    rate = kappa[...]

    def one_row(r):
        put_row(
            blocks, r,
            [flat[pl.ds(tile_row(r, x, columns), levels, stride=level_stride), :] for x in range(columns)],
            columns, levels,
        )

    def first_step(r):
        around = [row_of(blocks, r + i, columns, levels) for i in (-1, 0, 1)]
        put_row(stepped, r, stencil(rate, *around), columns, levels)

    done = 1
    for i, part in enumerate(parts):
        copies.wait(i)
        first, size = part.start * SUB, part.size * SUB
        loop(size, lambda r, first=first: one_row(first + r), unroll=size)
        last = first + size - 1
        loop(last - done, lambda r, done=done: first_step(done + r), unroll=last - done)
        done = last
    for i, r in enumerate((0, 1, rows - 2, rows - 1)):
        put_row(near, i, row_of(blocks, r, columns, levels), columns, levels)
    for i, r in enumerate((1, 2, rows - 3, rows - 2)):
        put_row(near, 4 + i, row_of(stepped, r, columns, levels), columns, levels)
    copies.wait("mask", "mix")
    for i, r in enumerate((0, 1, rows - 2, rows - 1)):
        mask_edge[i : i + 1, :] = mask[0, r : r + 1, :]
    mixing = mixing_of(mix[...])

    def second_step(i):
        r = i + 2
        around = [row_of(stepped, r + j, columns, levels) for j in (-1, 0, 1)]
        land = mask[0, pl.ds(r, 1), :].astype(F32)
        top, rest = column_physics(stencil(rate, *around), mixing, land)
        put_row(base, r, top, columns, NF)
        put_row(deep, r, rest, columns, depth)

    for first, last in ((0, rows - 20), (rows - 20, rows - 10), (rows - 10, rows - 4)):
        loop(last - first, lambda i, first=first: second_step(first + i), unroll=28)
        for name, source, target, size in (("base", base, base_out, NF), ("deep", deep, deep_out, depth)):
            middle = pl.ds((2 + first) * columns * size, (last - first) * columns * size)
            copies.start((name, first), source.at[middle], target.at[middle])
    copies.wait_all()


def edge_kernel(dims, kappa, near, mask_edge, mix, from_a, from_b, base_edge, deep, stepped, sems):
    _, columns, levels, tiles = dims
    tile = lax.axis_index("tile")
    even = lax.rem(tile, 2) == 0
    above_in = jnp.where(tile > 0, 1.0, 0.0).astype(F32)
    below_in = jnp.where(tile < tiles - 1, 1.0, 0.0).astype(F32)
    rate = kappa[...]
    mixing = mixing_of(mix[...])

    def slab_row(above, i):
        first, second = (from_b, from_a) if above else (from_a, from_b)
        return [
            jnp.where(even, p.astype(F32), q.astype(F32))
            for p, q in zip(
                row_of(first, i, columns, levels), row_of(second, i, columns, levels), strict=True
            )
        ]

    old = [row_of(near, i, columns, levels) for i in range(4)]
    above = [slab_row(True, i) for i in range(NSUB)]
    below = [slab_row(False, i) for i in range(NSUB)]
    new = [
        [v * above_in for v in stencil(rate, above[0], above[1], old[0])],
        stencil(rate, above[1], old[0], old[1]),
        stencil(rate, old[2], old[3], below[0]),
        [v * below_in for v in stencil(rate, old[3], below[0], below[1])],
    ]
    for i, values in enumerate(new):
        put_row(stepped, i, values, columns, levels)
    new = lambda i: row_of(stepped, i, columns, levels)
    at = lambda i: row_of(near, 4 + i, columns, levels)
    for i, around in enumerate(
        (
            (new(0), new(1), at(0)),
            (new(1), at(0), at(1)),
            (at(2), at(3), new(2)),
            (at(3), new(2), new(3)),
        )
    ):
        land = mask_edge[i : i + 1, :].astype(F32)
        top, rest = column_physics(stencil(rate, *around), mixing, land)
        put_row(base_edge, i, top, columns, NF)
        put_row(deep, i, rest, columns, levels - NF)


def surface_kernel(
    dims, arrived, base_edge, deep_edge, weight_in, dst_in, live_in_in, src_in, live_out_in, base_in, lagged_in, mask_in, weight_out_in,
    sent_out, top_out, flux_out, deep_edge_out,
    dst, live_in, src, live_out, base, lagged, mask, weight_out, sent, top, flux,
    numerator, denominator, sems,
):
    rows, columns, _, tiles = dims
    copies = Copies(sems)
    copies.start("dst", dst_in, dst)
    copies.start("live_in", live_in_in, live_in)
    tile_parts = parts_of(tiles, 4)
    middle = pl.ds(2 * columns * NF, (rows - 4) * columns * NF)
    copies.start("base", base_in.at[middle], base.at[middle])
    copies.start("lagged", lagged_in, lagged)
    copies.start("mask", mask_in, mask)
    copies.start("src", src_in, src)
    copies.start("live_out", live_out_in, live_out)
    for i, part in enumerate(tile_parts):
        copies.start(("weight_out", i), weight_out_in.at[part], weight_out.at[part])
    copies.start("deep_edge", deep_edge, deep_edge_out)
    comp = lax.axis_index("comp")
    other, own = (1 - comp) * tiles, comp * tiles

    def clear(r):
        for x in range(columns):
            where = pl.ds(aligned(r * columns + x, NF), NF)
            numerator[where, :] = jnp.zeros((NF, BLK), F32)
            denominator[where, :] = jnp.zeros((NF, BLK), F32)

    loop(rows, clear, unroll=32)
    ones = jnp.ones((NF, BLK), F32)

    def receive(t):
        got = arrived[other + t].astype(F32)
        for k in range(CAP):
            both = jnp.concatenate([got[k * NF : (k + 1) * NF], ones], axis=0).astype(BF16)
            product = jnp.dot(both, weight_in[t, k], preferred_element_type=F32)
            live = jnp.where(k < live_in[t], 1.0, 0.0).astype(F32)
            product = product * live
            where = pl.ds(aligned(dst[k, t], NF), NF)
            numerator[where, :] += product[:NF]
            denominator[where, :] += product[NF:]

    copies.wait("dst", "live_in")
    loop(tiles, receive, unroll=16)
    copies.wait("base", "lagged", "mask")
    atmosphere = jnp.where(comp == 0, 1.0, 0.0).astype(F32)

    def one_row(r, held=base, held_row=None):
        held_row = r if held_row is None else held_row
        land_row = mask[0, pl.ds(r, 1), :].astype(F32)
        for x in range(columns):
            where = pl.ds(aligned(r * columns + x, NF), NF)
            land = land_row[:, x * BLK : (x + 1) * BLK]
            received = numerator[where, :] / jnp.maximum(denominator[where, :], 1.0)
            before = lagged[pl.ds(tile_row(r, x, columns), NF, stride=rows * columns), :]
            incoming = before * atmosphere + received
            state = held[pl.ds(aligned(held_row * columns + x, NF), NF), :] + land * incoming
            top[where, :] = state
            flux[where, :] = land * jnp.tanh(state - incoming)

    loop(rows - 4, lambda i: one_row(i + 2), unroll=28)
    for i, r in enumerate((0, 1, rows - 2, rows - 1)):
        one_row(r, base_edge, i)
    copies.start("top", top, top_out)
    copies.start("flux", flux, flux_out)

    rows_of = lax.broadcasted_iota(jnp.int32, (SUB, BLK), 0)

    def send(t):
        sums = jnp.zeros((SUB, BLK), F32)
        for pair in range(CAP // 2):
            two = []
            for k in (2 * pair, 2 * pair + 1):
                picked = flux[pl.ds(aligned(src[k, t], NF), NF), :]
                both = jnp.concatenate([picked, ones], axis=0).astype(BF16)
                product = jnp.dot(both, weight_out[t, k], preferred_element_type=F32)
                product = product * jnp.where(k < live_out[t], 1.0, 0.0).astype(F32)
                two.append(product[:NF])
                sums = jnp.where((rows_of == k) | (rows_of == k + CAP), product[NF:], sums)
            both = jnp.concatenate(two, axis=0).astype(BF16)
            sent[other + t, pl.ds(2 * NF * pair, 2 * NF), :] = both
        high = sums.astype(BF16).astype(F32)
        sums = jnp.where(rows_of < CAP, high, sums - high)
        sums = jnp.concatenate([sums, jnp.zeros((SUB, BLK), F32)], axis=0)
        sent[own + t, pl.ds(0, 2 * SUB), :] = sums.astype(BF16)
        sent[own + t, pl.ds(2 * SUB, 2 * SUB), :] = jnp.zeros((2 * SUB, BLK), BF16)

    copies.wait("src", "live_out")
    copies.wait(*[("weight_out", i) for i in range(len(tile_parts))])
    for i, part in enumerate(parts_of(tiles, 2)):
        loop(part.size, lambda t, part=part: send(part.start + t), unroll=16)
        for half in (other, own):
            where = pl.ds(half + part.start, part.size)
            copies.start(("sent", i, half is own), sent.at[where], sent_out.at[where])
    copies.wait_all()


def write_kernel(dims, top_in, deep_in, deep_edge_in, flux_in, new_state_out, land_flux, top, deep, flux, new_state, sems):
    rows, columns, levels, _ = dims
    copies = Copies(sems)
    copies.start("top", top_in, top)
    depth = levels - NF
    row, two = columns * depth, 2 * columns * depth
    for name, source, first, target, size in (
        ("deep", deep_in, two, two, (rows - 4) * row),
        ("above", deep_edge_in, 0, 0, two),
        ("below", deep_edge_in, two, (rows - 2) * row, two),
    ):
        copies.start(name, source.at[pl.ds(first, size)], deep.at[pl.ds(target, size)])
    copies.start("flux", flux_in, flux)
    comp = lax.axis_index("comp")
    on_land = jnp.where(comp == 1, 1.0, 0.0).astype(F32)
    cut = NF * rows * columns

    def from_blocks(source, target, count, first, scale=None):
        def one(rt):
            for x in range(columns):
                for level in range(count):
                    out = ((level + first) * (rows // SUB) + rt) * columns + x
                    start = (rt * SUB * columns + x) * count + level
                    value = source[pl.ds(start, SUB, stride=columns * count), :]
                    value = value if scale is None else value * scale
                    target[pl.ds(aligned(out, SUB), SUB), :] = value

        loop(rows // SUB, one, unroll=4)

    copies.wait("top")
    from_blocks(top, new_state, NF, 0)
    copies.start("state", new_state.at[pl.ds(0, cut)], new_state_out.at[pl.ds(0, cut)])
    copies.wait("deep", "above", "below")
    from_blocks(deep, new_state, depth, NF)
    rest = pl.ds(cut, depth * rows * columns)
    copies.start("rest", new_state.at[rest], new_state_out.at[rest])
    copies.wait("flux")
    from_blocks(flux, land_flux, NF, 0, on_land)
    copies.wait_all()


def return_kernel(dims, arrived, land_flux, dst_in, fluxes_out, dst, fluxes, numerator, denominator, sems):
    rows, columns, _, tiles = dims
    copies = Copies(sems)
    copies.start("dst", dst_in, dst)
    halves = parts_of(NF * rows * columns, 2)
    for i, part in enumerate(halves):
        copies.start(i, land_flux.at[part], fluxes.at[part])
    comp = lax.axis_index("comp")
    other = (1 - comp) * tiles
    level_stride = rows * columns

    def clear(r):
        for x in range(columns):
            where = pl.ds(aligned(r * columns + x, NF), NF)
            numerator[where, :] = jnp.zeros((NF, BLK), F32)
            denominator[where, :] = jnp.zeros((NF, BLK), F32)

    loop(rows, clear, unroll=32)

    def receive(t):
        got = arrived[other + t].astype(F32)
        sums = arrived[comp * tiles + t].astype(F32)
        sums = sums[:CAP] + sums[CAP : 2 * CAP]
        for k in range(CAP):
            where = pl.ds(aligned(dst[k, t], NF), NF)
            numerator[where, :] += got[k * NF : (k + 1) * NF]
            denominator[where, :] += jnp.broadcast_to(sums[k : k + 1], (NF, BLK))

    copies.wait("dst")
    loop(tiles, receive, unroll=16)
    copies.wait_all()

    def finish(t):
        for k in range(CAP):
            block = dst[k, t]
            where = pl.ds(aligned(block, NF), NF)
            out = pl.ds(block_tile_row(block, columns), NF, stride=level_stride)
            value = numerator[where, :] / jnp.maximum(denominator[where, :], 1.0)
            fluxes[out, :] = land_flux[out, :] + value

    loop(tiles, finish, unroll=16)
    for i, part in enumerate(halves):
        copies.start(("out", i), fluxes.at[part], fluxes_out.at[part])
    copies.wait_all()


def call(kernel, operands, places, outs, scratch, copies, limit, cost):
    vmem, hbm = pl.BlockSpec(memory_space=pltpu.VMEM), pl.BlockSpec(memory_space=pltpu.HBM)
    spec = {"v": vmem, "m": vmem, "h": hbm}
    space = {"m": pltpu.VMEM, "h": pltpu.HBM}
    operands = [
        pltpu.with_memory_space_constraint(x, space[place]) if place in space else x
        for x, place in zip(operands, places, strict=True)
    ]
    return pl.pallas_call(
        kernel,
        out_shape=[out for out, _ in outs],
        in_specs=[spec[place] for place in places],
        out_specs=[spec[place] for _, place in outs],
        scratch_shapes=[*scratch, pltpu.SemaphoreType.DMA((copies,))],
        compiler_params=pltpu.CompilerParams(vmem_limit_bytes=limit),
        cost_estimate=pl.CostEstimate(flops=cost, bytes_accessed=cost // 4, transcendentals=0),
    )(*operands)


def per_device(
    state,
    kappa,
    col_mix,
    surface_mask,
    lagged_flux,
    a2l_src,
    a2l_dst,
    a2l_count,
    a2l_weight,
    l2a_src,
    l2a_dst,
    l2a_count,
    l2a_weight,
):
    fields = state[0]
    levels, rows, cells = fields.shape
    columns = cells // BLK
    nblocks = rows * columns
    tiles = lax.axis_size("tile")
    dims = (rows, columns, levels, tiles)
    shape, vmem, smem = pltpu.HBM, pltpu.VMEM, pltpu.SMEM
    kernel = lambda f: functools.partial(f, dims)
    limit = VMEM_LIMIT + 4 * tiles * CAP * BLK * BLK
    state_tiles = tile_view(fields)
    slab = (NSUB * columns * levels, BLK)
    parcel = (2 * tiles, CAP * NF, BLK)
    top_shape = (nblocks * NF, BLK)
    deep_shape = (nblocks * (levels - NF), BLK)
    full_shape = (nblocks * levels, BLK)
    weight_shape = (tiles, CAP, BLK, BLK)
    slots, counts = smem((CAP, tiles), jnp.int32), smem((tiles,), jnp.int32)
    sent, slab_a, slab_b = call(
        kernel(pick_kernel), [a2l_src[:, 0, :].T, state_tiles], "hh",
        [(shape(parcel, BF16), "h"), (vmem(slab, BF16), "v"), (vmem(slab, BF16), "v")],
        [slots, vmem(full_shape, F32), vmem(parcel, BF16)],
        8, limit, 4_000_000,
    )
    arrived = lax.all_to_all(sent, ("comp", "tile"), split_axis=0, concat_axis=0, tiled=True)
    from_a = lax.ppermute(slab_a, "tile", [(i, i ^ 1) for i in range(tiles)])
    pairs = [(i, i + 1) for i in range(1, tiles - 1, 2)]
    from_b = lax.ppermute(slab_b, "tile", pairs + [(j, i) for i, j in pairs])
    rates = jnp.broadcast_to(kappa[0][:, None], (levels, BLK))
    near, base, deep, mask_edge, mix, weight_in = call(
        kernel(inner_kernel),
        [rates, state_tiles.reshape(levels, nblocks, BLK), surface_mask, col_mix[0], a2l_weight[0]], "vhhhh",
        [(vmem((8 * columns * levels, BLK), F32), "v"), (shape(top_shape, F32), "h"),
         (shape(deep_shape, F32), "h"), (vmem((4, cells), jnp.int32), "v"),
         (vmem((levels, levels), F32), "v"), (vmem(weight_shape, BF16), "v")],
        [vmem((1, rows, cells), jnp.int32), vmem((levels, nblocks, BLK), F32), vmem(full_shape, F32),
         vmem(full_shape, F32), vmem(top_shape, F32), vmem(deep_shape, F32)],
        16, limit, 20_000_000,
    )
    base_edge, deep_near = call(
        kernel(edge_kernel), [rates, near, mask_edge, mix, from_a, from_b], "vvvvvv",
        [(vmem((4 * columns * NF, BLK), F32), "v"), (vmem((4 * columns * (levels - NF), BLK), F32), "v")],
        [vmem((4 * columns * levels, BLK), F32)],
        1, limit, 4_000_000,
    )
    sent_back, top, flux, deep_edge = call(
        kernel(surface_kernel),
        [arrived, base_edge, deep_near, weight_in, a2l_dst[0].T, a2l_count[0], l2a_src[:, 0, :].T,
         l2a_count[:, 0], base, tile_view(lagged_flux), surface_mask, l2a_weight[:, 0]], "vvvvhhhhhhhh",
        [(shape(parcel, BF16), "h"), (shape(top_shape, F32), "h"), (shape(top_shape, F32), "h"),
         (shape((4 * columns * (levels - NF), BLK), F32), "h")],
        [slots, counts, slots, counts, vmem(top_shape, F32), vmem(top_shape, F32), vmem((1, rows, cells), jnp.int32),
         vmem(weight_shape, BF16), vmem(parcel, BF16), vmem(top_shape, F32), vmem(top_shape, F32), vmem(top_shape, F32), vmem(top_shape, F32)],
        23, limit, 20_000_000,
    )
    returned = lax.all_to_all(
        sent_back, ("comp", "tile"), split_axis=0, concat_axis=0, tiled=True
    )
    new_state, land_flux = call(
        kernel(write_kernel), [top, deep, deep_edge, flux], "hhhh",
        [(shape(full_shape, F32), "h"), (vmem(top_shape, F32), "v")],
        [vmem(top_shape, F32), vmem(deep_shape, F32), vmem(top_shape, F32), vmem(full_shape, F32),
         ],
        8, limit, 20_000_000,
    )
    (fluxes,) = call(
        kernel(return_kernel), [returned, land_flux, l2a_dst[0].T], "vvm",
        [(shape(top_shape, F32), "h")],
        [slots, vmem(top_shape, F32), vmem(top_shape, F32), vmem(top_shape, F32)],
        6, limit, 10_000_000,
    )
    return (
        from_tile_view(new_state, levels, rows, cells)[None],
        from_tile_view(fluxes, NF, rows, cells)[None],
    )


def solution(mesh):
    return jax.shard_map(
        per_device,
        mesh=mesh,
        in_specs=(
            P("comp", None, "tile", None),
            P("comp", None),
            P("comp", None, None),
            P("comp", "tile", None),
            P(None, "tile", None),
            P(None, "tile", None),
            P("tile", None, None),
            P("tile", None),
            P("tile", None, None, None, None),
            P(None, "tile", None),
            P("tile", None, None),
            P(None, "tile"),
            P(None, "tile", None, None, None),
        ),
        out_specs=(P("comp", None, "tile", None), P("comp", None, "tile", None)),
        check_vma=False,
    )
```

```python
import functools

import jax
import jax.numpy as jnp
from jax import lax
from jax.experimental import pallas as pl
from jax.experimental.pallas import tpu as pltpu
from jax.sharding import PartitionSpec as P


NF = 8
BLK = 128
CAP = 4
NSUB = 2
SUB = 8
F32 = jnp.float32
BF16 = jnp.bfloat16
VMEM_LIMIT = 12 * 1024 * 1024


def tile_view(grid):
    levels, rows, cells = grid.shape
    split = grid.reshape(levels, rows // SUB, SUB, cells // BLK, BLK)
    return split.transpose(0, 1, 3, 2, 4).reshape(levels * rows * cells // BLK, BLK)


def from_tile_view(tiles, levels, rows, cells):
    split = tiles.reshape(levels, rows // SUB, cells // BLK, SUB, BLK)
    return split.transpose(0, 1, 3, 2, 4).reshape(levels, rows, cells)


def tile_row(row, x, columns):
    return (lax.div(row, SUB) * columns + x) * SUB + lax.rem(row, SUB)


def block_tile_row(block, columns):
    return tile_row(lax.div(block, columns), lax.rem(block, columns), columns)


def aligned(index, step):
    return pl.multiple_of(index * step, step)


def loop(count, body, unroll=1):
    def step(i, carry):
        body(i)
        return carry

    lax.fori_loop(0, count, step, 0, unroll=min(unroll, count))


class Copies:
    def __init__(self, semaphores):
        self.semaphores, self.open, self.used = semaphores, {}, 0

    def start(self, name, source, target):
        copy = pltpu.make_async_copy(source, target, self.semaphores.at[self.used])
        self.used += 1
        copy.start()
        self.open[name] = copy

    def wait(self, *names):
        for name in names:
            self.open.pop(name).wait()

    def wait_all(self):
        self.wait(*list(self.open))


def parts_of(count, parts):
    parts = parts if count % parts == 0 else 1
    return [pl.ds(i * (count // parts), count // parts) for i in range(parts)]


def pick_kernel(dims, src_in, state_in, sent_out, slab_a, slab_b, src, state, sent, sems):
    rows, columns, levels, tiles = dims
    copies = Copies(sems)
    level_stride = rows * columns
    copies.start("src", src_in, src)
    for i, part in enumerate(parts_of(NF * level_stride, 4)):
        copies.start(("top", i), state_in.at[part], state.at[part])
    deep = pl.ds(NF * level_stride, (levels - NF) * level_stride)
    copies.start("deep", state_in.at[deep], state.at[deep])
    comp, tile = lax.axis_index("comp"), lax.axis_index("tile")
    other = (1 - comp) * tiles

    def blank(t):
        sent[comp * tiles + t] = jnp.zeros((CAP * NF, BLK), BF16)

    loop(tiles, blank, unroll=16)

    def one_tile(t):
        for pair in range(CAP // 2):
            two = []
            for k in (2 * pair, 2 * pair + 1):
                start = block_tile_row(src[k, t], columns)
                two.append(state[pl.ds(start, NF, stride=level_stride), :])
            both = jnp.concatenate(two, axis=0).astype(BF16)
            sent[other + t, pl.ds(2 * NF * pair, 2 * NF), :] = both

    copies.wait("src", *[("top", i) for i in range(len(parts_of(NF * level_stride, 4)))])
    loop(tiles, one_tile, unroll=16)
    for name, half in (("sent", other), ("own", comp * tiles)):
        where = pl.ds(half, tiles)
        copies.start(name, sent.at[where], sent_out.at[where])
    even = lax.rem(tile, 2) == 0
    copies.wait("deep")
    for slab, first in (
        (slab_a, jnp.where(even, rows - NSUB, 0)),
        (slab_b, jnp.where(even, 0, rows - NSUB)),
    ):
        for i in range(NSUB):
            for x in range(columns):
                start = tile_row(first + i, x, columns)
                value = state[pl.ds(start, levels, stride=level_stride), :]
                slab[(i * columns + x) * levels : (i * columns + x + 1) * levels, :] = value.astype(BF16)
    copies.wait_all()


def row_of(ref, r, columns, levels):
    return [ref[pl.ds(aligned(r * columns + x, levels), levels), :] for x in range(columns)]


def rows_of_tile(ref, rt, x, columns, level_stride, levels):
    tall = []
    for half in range(levels // SUB):
        tiles = []
        for level in range(half * SUB, (half + 1) * SUB):
            start = pl.multiple_of(level * level_stride + (rt * columns + x) * SUB, SUB)
            tiles.append(ref[pl.ds(start, SUB), :])
        tall.append(jnp.transpose(jnp.stack(tiles), (1, 0, 2)))
    return [jnp.concatenate([t[i] for t in tall], axis=0) for i in range(SUB)]


def put_row(ref, r, values, columns, levels):
    for x, v in enumerate(values):
        ref[pl.ds(aligned(r * columns + x, levels), levels), :] = v


def stencil(rate, up, mid, down):
    columns = len(mid)
    keep = 1.0 - 4.0 * rate
    lane = lax.broadcasted_iota(jnp.int32, rate.shape, 1)
    right_roll = [pltpu.roll(v, 1, 1) for v in mid]
    left_roll = [pltpu.roll(v, BLK - 1, 1) for v in mid]
    out = []
    for x in range(columns):
        west = jnp.where(lane == 0, right_roll[x - 1], right_roll[x])
        east = jnp.where(lane == BLK - 1, left_roll[(x + 1) % columns], left_roll[x])
        out.append(keep * mid[x] + rate * (up[x] + down[x] + (west + east)))
    return out


def mixing_of(col_mix):
    mix_high = col_mix.astype(BF16)
    mix_low = (col_mix - mix_high.astype(F32)).astype(BF16)
    return jnp.concatenate([mix_high, mix_high, mix_low], axis=1)


def column_physics(diffused, mixing, land):
    whole = jnp.concatenate(diffused, axis=1)
    high = whole.astype(BF16)
    low = (whole - high.astype(F32)).astype(BF16)
    three = jnp.concatenate([high, low, high], axis=0)
    moved = whole + 0.5 * jnp.tanh(jnp.dot(mixing, three, preferred_element_type=F32))
    top = moved[:NF] - (0.5 * (1.0 - land)) * whole[:NF]
    columns = len(diffused)
    cut = lambda v: [v[:, x * BLK : (x + 1) * BLK] for x in range(columns)]
    return cut(top), cut(moved[NF:])


def inner_kernel(
    dims, kappa, state_in, mask_in, mix_in, weight_in, near, base_out, deep_out, mask_edge, mix, weight,
    mask, state, blocks, stepped, base, deep, sems,
):
    rows, columns, levels, _ = dims
    depth = levels - NF
    copies = Copies(sems)
    level_stride = rows * columns
    parts = parts_of(rows // SUB, 4)
    for i, part in enumerate(parts):
        where = pl.ds(part.start * columns * SUB, part.size * columns * SUB)
        copies.start(i, state_in.at[:, where], state.at[:, where])
    copies.start("mask", mask_in, mask)
    copies.start("mix", mix_in, mix)
    copies.start("weight", weight_in, weight)
    flat = state.reshape(levels * level_stride, BLK)
    rate = kappa[...]

    def one_tile_row(rt):
        for x in range(columns):
            for i, value in enumerate(rows_of_tile(flat, rt, x, columns, level_stride, levels)):
                where = (rt * SUB + i) * columns + x
                blocks[pl.ds(aligned(where, levels), levels), :] = value

    def first_step(r):
        around = [row_of(blocks, r + i, columns, levels) for i in (-1, 0, 1)]
        put_row(stepped, r, stencil(rate, *around), columns, levels)

    done = 1
    for i, part in enumerate(parts):
        copies.wait(i)
        first, size = part.start * SUB, part.size * SUB
        loop(part.size, lambda rt, part=part: one_tile_row(part.start + rt), unroll=part.size)
        last = first + size - 1
        loop(last - done, lambda r, done=done: first_step(done + r), unroll=last - done)
        done = last
    for i, r in enumerate((0, 1, rows - 2, rows - 1)):
        put_row(near, i, row_of(blocks, r, columns, levels), columns, levels)
    for i, r in enumerate((1, 2, rows - 3, rows - 2)):
        put_row(near, 4 + i, row_of(stepped, r, columns, levels), columns, levels)
    copies.wait("mask", "mix")
    for i, r in enumerate((0, 1, rows - 2, rows - 1)):
        mask_edge[i : i + 1, :] = mask[0, r : r + 1, :]
    mixing = mixing_of(mix[...])

    def second_step(i):
        r = i + 2
        around = [row_of(stepped, r + j, columns, levels) for j in (-1, 0, 1)]
        land = mask[0, pl.ds(r, 1), :].astype(F32)
        top, rest = column_physics(stencil(rate, *around), mixing, land)
        put_row(base, r, top, columns, NF)
        put_row(deep, r, rest, columns, depth)

    for first, last in ((0, rows - 20), (rows - 20, rows - 10), (rows - 10, rows - 4)):
        loop(last - first, lambda i, first=first: second_step(first + i), unroll=28)
        for name, source, target, size in (("base", base, base_out, NF), ("deep", deep, deep_out, depth)):
            middle = pl.ds((2 + first) * columns * size, (last - first) * columns * size)
            copies.start((name, first), source.at[middle], target.at[middle])
    copies.wait_all()


def edge_kernel(dims, kappa, near, mask_edge, mix, from_a, from_b, base_edge, deep, stepped, sems):
    _, columns, levels, tiles = dims
    tile = lax.axis_index("tile")
    even = lax.rem(tile, 2) == 0
    above_in = jnp.where(tile > 0, 1.0, 0.0).astype(F32)
    below_in = jnp.where(tile < tiles - 1, 1.0, 0.0).astype(F32)
    rate = kappa[...]
    mixing = mixing_of(mix[...])

    def slab_row(above, i):
        first, second = (from_b, from_a) if above else (from_a, from_b)
        return [
            jnp.where(even, p.astype(F32), q.astype(F32))
            for p, q in zip(
                row_of(first, i, columns, levels), row_of(second, i, columns, levels), strict=True
            )
        ]

    old = [row_of(near, i, columns, levels) for i in range(4)]
    above = [slab_row(True, i) for i in range(NSUB)]
    below = [slab_row(False, i) for i in range(NSUB)]
    new = [
        [v * above_in for v in stencil(rate, above[0], above[1], old[0])],
        stencil(rate, above[1], old[0], old[1]),
        stencil(rate, old[2], old[3], below[0]),
        [v * below_in for v in stencil(rate, old[3], below[0], below[1])],
    ]
    for i, values in enumerate(new):
        put_row(stepped, i, values, columns, levels)
    new = lambda i: row_of(stepped, i, columns, levels)
    at = lambda i: row_of(near, 4 + i, columns, levels)
    for i, around in enumerate(
        (
            (new(0), new(1), at(0)),
            (new(1), at(0), at(1)),
            (at(2), at(3), new(2)),
            (at(3), new(2), new(3)),
        )
    ):
        land = mask_edge[i : i + 1, :].astype(F32)
        top, rest = column_physics(stencil(rate, *around), mixing, land)
        put_row(base_edge, i, top, columns, NF)
        put_row(deep, i, rest, columns, levels - NF)


def surface_kernel(
    dims, arrived, base_edge, deep_edge, weight_in, dst_in, live_in_in, src_in, live_out_in, base_in, lagged_in, mask_in, weight_out_in,
    sent_out, top_out, flux_out, deep_edge_out,
    dst, live_in, src, live_out, base, lagged, mask, weight_out, sent, top, flux,
    numerator, denominator, sems,
):
    rows, columns, _, tiles = dims
    copies = Copies(sems)
    copies.start("dst", dst_in, dst)
    copies.start("live_in", live_in_in, live_in)
    tile_parts = parts_of(tiles, 4)
    middle = pl.ds(2 * columns * NF, (rows - 4) * columns * NF)
    copies.start("base", base_in.at[middle], base.at[middle])
    copies.start("lagged", lagged_in, lagged)
    copies.start("mask", mask_in, mask)
    copies.start("src", src_in, src)
    copies.start("live_out", live_out_in, live_out)
    for i, part in enumerate(tile_parts):
        copies.start(("weight_out", i), weight_out_in.at[part], weight_out.at[part])
    copies.start("deep_edge", deep_edge, deep_edge_out)
    comp = lax.axis_index("comp")
    other, own = (1 - comp) * tiles, comp * tiles

    def clear(r):
        for x in range(columns):
            where = pl.ds(aligned(r * columns + x, NF), NF)
            numerator[where, :] = jnp.zeros((NF, BLK), F32)
            denominator[where, :] = jnp.zeros((NF, BLK), F32)

    loop(rows, clear, unroll=32)
    ones = jnp.ones((NF, BLK), F32)

    def receive(t):
        got = arrived[other + t].astype(F32)
        for k in range(CAP):
            both = jnp.concatenate([got[k * NF : (k + 1) * NF], ones], axis=0).astype(BF16)
            product = jnp.dot(both, weight_in[t, k], preferred_element_type=F32)
            live = jnp.where(k < live_in[t], 1.0, 0.0).astype(F32)
            product = product * live
            where = pl.ds(aligned(dst[k, t], NF), NF)
            numerator[where, :] += product[:NF]
            denominator[where, :] += product[NF:]

    copies.wait("dst", "live_in")
    loop(tiles, receive, unroll=16)
    copies.wait("lagged")
    atmosphere = jnp.where(comp == 0, 1.0, 0.0).astype(F32)

    def earlier(rt):
        for x in range(columns):
            for i, value in enumerate(rows_of_tile(lagged, rt, x, columns, rows * columns, NF)):
                where = (rt * SUB + i) * columns + x
                top[pl.ds(aligned(where, NF), NF), :] = value * atmosphere

    loop(rows // SUB, earlier, unroll=4)
    copies.wait("base", "mask")

    def one_row(r, held=base, held_row=None):
        held_row = r if held_row is None else held_row
        land_row = mask[0, pl.ds(r, 1), :].astype(F32)
        for x in range(columns):
            where = pl.ds(aligned(r * columns + x, NF), NF)
            land = land_row[:, x * BLK : (x + 1) * BLK]
            received = numerator[where, :] / jnp.maximum(denominator[where, :], 1.0)
            incoming = top[where, :] + received
            state = held[pl.ds(aligned(held_row * columns + x, NF), NF), :] + land * incoming
            top[where, :] = state
            flux[where, :] = land * jnp.tanh(state - incoming)

    loop(rows - 4, lambda i: one_row(i + 2), unroll=28)
    for i, r in enumerate((0, 1, rows - 2, rows - 1)):
        one_row(r, base_edge, i)
    copies.start("top", top, top_out)
    copies.start("flux", flux, flux_out)

    rows_of = lax.broadcasted_iota(jnp.int32, (SUB, BLK), 0)

    def send(t):
        sums = jnp.zeros((SUB, BLK), F32)
        for pair in range(CAP // 2):
            two = []
            for k in (2 * pair, 2 * pair + 1):
                picked = flux[pl.ds(aligned(src[k, t], NF), NF), :]
                both = jnp.concatenate([picked, ones], axis=0).astype(BF16)
                product = jnp.dot(both, weight_out[t, k], preferred_element_type=F32)
                product = product * jnp.where(k < live_out[t], 1.0, 0.0).astype(F32)
                two.append(product[:NF])
                sums = jnp.where((rows_of == k) | (rows_of == k + CAP), product[NF:], sums)
            both = jnp.concatenate(two, axis=0).astype(BF16)
            sent[other + t, pl.ds(2 * NF * pair, 2 * NF), :] = both
        high = sums.astype(BF16).astype(F32)
        sums = jnp.where(rows_of < CAP, high, sums - high)
        sums = jnp.concatenate([sums, jnp.zeros((SUB, BLK), F32)], axis=0)
        sent[own + t, pl.ds(0, 2 * SUB), :] = sums.astype(BF16)
        sent[own + t, pl.ds(2 * SUB, 2 * SUB), :] = jnp.zeros((2 * SUB, BLK), BF16)

    copies.wait("src", "live_out")
    copies.wait(*[("weight_out", i) for i in range(len(tile_parts))])
    for i, part in enumerate(parts_of(tiles, 2)):
        loop(part.size, lambda t, part=part: send(part.start + t), unroll=16)
        for half in (other, own):
            where = pl.ds(half + part.start, part.size)
            copies.start(("sent", i, half is own), sent.at[where], sent_out.at[where])
    copies.wait_all()


def write_kernel(dims, top_in, deep_in, deep_edge_in, flux_in, new_state_out, land_flux, top, deep, flux, new_state, sems):
    rows, columns, levels, _ = dims
    copies = Copies(sems)
    copies.start("top", top_in, top)
    depth = levels - NF
    row, two = columns * depth, 2 * columns * depth
    for name, source, first, target, size in (
        ("deep", deep_in, two, two, (rows - 4) * row),
        ("above", deep_edge_in, 0, 0, two),
        ("below", deep_edge_in, two, (rows - 2) * row, two),
    ):
        copies.start(name, source.at[pl.ds(first, size)], deep.at[pl.ds(target, size)])
    copies.start("flux", flux_in, flux)
    comp = lax.axis_index("comp")
    on_land = jnp.where(comp == 1, 1.0, 0.0).astype(F32)
    cut = NF * rows * columns

    def from_blocks(source, target, count, first, scale=None):
        def one(rt):
            for x in range(columns):
                for level in range(count):
                    out = ((level + first) * (rows // SUB) + rt) * columns + x
                    start = (rt * SUB * columns + x) * count + level
                    value = source[pl.ds(start, SUB, stride=columns * count), :]
                    value = value if scale is None else value * scale
                    target[pl.ds(aligned(out, SUB), SUB), :] = value

        loop(rows // SUB, one, unroll=4)

    copies.wait("top")
    from_blocks(top, new_state, NF, 0)
    copies.start("state", new_state.at[pl.ds(0, cut)], new_state_out.at[pl.ds(0, cut)])
    copies.wait("deep", "above", "below")
    from_blocks(deep, new_state, depth, NF)
    rest = pl.ds(cut, depth * rows * columns)
    copies.start("rest", new_state.at[rest], new_state_out.at[rest])
    copies.wait("flux")
    from_blocks(flux, land_flux, NF, 0, on_land)
    copies.wait_all()


def return_kernel(dims, arrived, land_flux, dst_in, fluxes_out, dst, fluxes, numerator, denominator, sems):
    rows, columns, _, tiles = dims
    copies = Copies(sems)
    copies.start("dst", dst_in, dst)
    halves = parts_of(NF * rows * columns, 2)
    for i, part in enumerate(halves):
        copies.start(i, land_flux.at[part], fluxes.at[part])
    comp = lax.axis_index("comp")
    other = (1 - comp) * tiles
    level_stride = rows * columns

    def clear(r):
        for x in range(columns):
            where = pl.ds(aligned(r * columns + x, NF), NF)
            numerator[where, :] = jnp.zeros((NF, BLK), F32)
            denominator[where, :] = jnp.zeros((NF, BLK), F32)

    loop(rows, clear, unroll=32)

    def receive(t):
        got = arrived[other + t].astype(F32)
        sums = arrived[comp * tiles + t].astype(F32)
        sums = sums[:CAP] + sums[CAP : 2 * CAP]
        for k in range(CAP):
            where = pl.ds(aligned(dst[k, t], NF), NF)
            numerator[where, :] += got[k * NF : (k + 1) * NF]
            denominator[where, :] += jnp.broadcast_to(sums[k : k + 1], (NF, BLK))

    copies.wait("dst")
    loop(tiles, receive, unroll=16)
    copies.wait_all()

    def finish(t):
        for k in range(CAP):
            block = dst[k, t]
            where = pl.ds(aligned(block, NF), NF)
            out = pl.ds(block_tile_row(block, columns), NF, stride=level_stride)
            value = numerator[where, :] / jnp.maximum(denominator[where, :], 1.0)
            fluxes[out, :] = land_flux[out, :] + value

    loop(tiles, finish, unroll=16)
    for i, part in enumerate(halves):
        copies.start(("out", i), fluxes.at[part], fluxes_out.at[part])
    copies.wait_all()


def call(kernel, operands, places, outs, scratch, copies, limit, cost):
    vmem, hbm = pl.BlockSpec(memory_space=pltpu.VMEM), pl.BlockSpec(memory_space=pltpu.HBM)
    spec = {"v": vmem, "m": vmem, "h": hbm}
    space = {"m": pltpu.VMEM, "h": pltpu.HBM}
    operands = [
        pltpu.with_memory_space_constraint(x, space[place]) if place in space else x
        for x, place in zip(operands, places, strict=True)
    ]
    return pl.pallas_call(
        kernel,
        out_shape=[out for out, _ in outs],
        in_specs=[spec[place] for place in places],
        out_specs=[spec[place] for _, place in outs],
        scratch_shapes=[*scratch, pltpu.SemaphoreType.DMA((copies,))],
        compiler_params=pltpu.CompilerParams(vmem_limit_bytes=limit),
        cost_estimate=pl.CostEstimate(flops=cost, bytes_accessed=cost // 4, transcendentals=0),
    )(*operands)


def per_device(
    state,
    kappa,
    col_mix,
    surface_mask,
    lagged_flux,
    a2l_src,
    a2l_dst,
    a2l_count,
    a2l_weight,
    l2a_src,
    l2a_dst,
    l2a_count,
    l2a_weight,
):
    fields = state[0]
    levels, rows, cells = fields.shape
    columns = cells // BLK
    nblocks = rows * columns
    tiles = lax.axis_size("tile")
    dims = (rows, columns, levels, tiles)
    shape, vmem, smem = pltpu.HBM, pltpu.VMEM, pltpu.SMEM
    kernel = lambda f: functools.partial(f, dims)
    limit = VMEM_LIMIT + 4 * tiles * CAP * BLK * BLK
    state_tiles = tile_view(fields)
    slab = (NSUB * columns * levels, BLK)
    parcel = (2 * tiles, CAP * NF, BLK)
    top_shape = (nblocks * NF, BLK)
    deep_shape = (nblocks * (levels - NF), BLK)
    full_shape = (nblocks * levels, BLK)
    weight_shape = (tiles, CAP, BLK, BLK)
    slots, counts = smem((CAP, tiles), jnp.int32), smem((tiles,), jnp.int32)
    sent, slab_a, slab_b = call(
        kernel(pick_kernel), [a2l_src[:, 0, :].T, state_tiles], "hh",
        [(shape(parcel, BF16), "h"), (vmem(slab, BF16), "v"), (vmem(slab, BF16), "v")],
        [slots, vmem(full_shape, F32), vmem(parcel, BF16)],
        8, limit, 4_000_000,
    )
    arrived = lax.all_to_all(sent, ("comp", "tile"), split_axis=0, concat_axis=0, tiled=True)
    from_a = lax.ppermute(slab_a, "tile", [(i, i ^ 1) for i in range(tiles)])
    pairs = [(i, i + 1) for i in range(1, tiles - 1, 2)]
    from_b = lax.ppermute(slab_b, "tile", pairs + [(j, i) for i, j in pairs])
    rates = jnp.broadcast_to(kappa[0][:, None], (levels, BLK))
    near, base, deep, mask_edge, mix, weight_in = call(
        kernel(inner_kernel),
        [rates, state_tiles.reshape(levels, nblocks, BLK), surface_mask, col_mix[0], a2l_weight[0]], "vhhhh",
        [(vmem((8 * columns * levels, BLK), F32), "v"), (shape(top_shape, F32), "h"),
         (shape(deep_shape, F32), "h"), (vmem((4, cells), jnp.int32), "v"),
         (vmem((levels, levels), F32), "v"), (vmem(weight_shape, BF16), "v")],
        [vmem((1, rows, cells), jnp.int32), vmem((levels, nblocks, BLK), F32), vmem(full_shape, F32),
         vmem(full_shape, F32), vmem(top_shape, F32), vmem(deep_shape, F32)],
        16, limit, 20_000_000,
    )
    base_edge, deep_near = call(
        kernel(edge_kernel), [rates, near, mask_edge, mix, from_a, from_b], "vvvvvv",
        [(vmem((4 * columns * NF, BLK), F32), "v"), (vmem((4 * columns * (levels - NF), BLK), F32), "v")],
        [vmem((4 * columns * levels, BLK), F32)],
        1, limit, 4_000_000,
    )
    sent_back, top, flux, deep_edge = call(
        kernel(surface_kernel),
        [arrived, base_edge, deep_near, weight_in, a2l_dst[0].T, a2l_count[0], l2a_src[:, 0, :].T,
         l2a_count[:, 0], base, tile_view(lagged_flux), surface_mask, l2a_weight[:, 0]], "vvvvhhhhhhhh",
        [(shape(parcel, BF16), "h"), (shape(top_shape, F32), "h"), (shape(top_shape, F32), "h"),
         (shape((4 * columns * (levels - NF), BLK), F32), "h")],
        [slots, counts, slots, counts, vmem(top_shape, F32), vmem(top_shape, F32), vmem((1, rows, cells), jnp.int32),
         vmem(weight_shape, BF16), vmem(parcel, BF16), vmem(top_shape, F32), vmem(top_shape, F32), vmem(top_shape, F32), vmem(top_shape, F32)],
        23, limit, 20_000_000,
    )
    returned = lax.all_to_all(
        sent_back, ("comp", "tile"), split_axis=0, concat_axis=0, tiled=True
    )
    new_state, land_flux = call(
        kernel(write_kernel), [top, deep, deep_edge, flux], "hhhh",
        [(shape(full_shape, F32), "h"), (vmem(top_shape, F32), "v")],
        [vmem(top_shape, F32), vmem(deep_shape, F32), vmem(top_shape, F32), vmem(full_shape, F32),
         ],
        8, limit, 20_000_000,
    )
    (fluxes,) = call(
        kernel(return_kernel), [returned, land_flux, l2a_dst[0].T], "vvm",
        [(shape(top_shape, F32), "h")],
        [slots, vmem(top_shape, F32), vmem(top_shape, F32), vmem(top_shape, F32)],
        6, limit, 10_000_000,
    )
    return (
        from_tile_view(new_state, levels, rows, cells)[None],
        from_tile_view(fluxes, NF, rows, cells)[None],
    )


def solution(mesh):
    return jax.shard_map(
        per_device,
        mesh=mesh,
        in_specs=(
            P("comp", None, "tile", None),
            P("comp", None),
            P("comp", None, None),
            P("comp", "tile", None),
            P(None, "tile", None),
            P(None, "tile", None),
            P("tile", None, None),
            P("tile", None),
            P("tile", None, None, None, None),
            P(None, "tile", None),
            P("tile", None, None),
            P(None, "tile"),
            P(None, "tile", None, None, None),
        ),
        out_specs=(P("comp", None, "tile", None), P("comp", None, "tile", None)),
        check_vma=False,
    )
```

```python
import functools

import jax
import jax.numpy as jnp
from jax import lax
from jax.experimental import pallas as pl
from jax.experimental.pallas import tpu as pltpu
from jax.sharding import PartitionSpec as P


NF = 8
BLK = 128
CAP = 4
NSUB = 2
SUB = 8
F32 = jnp.float32
BF16 = jnp.bfloat16
VMEM_LIMIT = 12 * 1024 * 1024


def tile_view(grid):
    levels, rows, cells = grid.shape
    split = grid.reshape(levels, rows // SUB, SUB, cells // BLK, BLK)
    return split.transpose(0, 1, 3, 2, 4).reshape(levels * rows * cells // BLK, BLK)


def from_tile_view(tiles, levels, rows, cells):
    split = tiles.reshape(levels, rows // SUB, cells // BLK, SUB, BLK)
    return split.transpose(0, 1, 3, 2, 4).reshape(levels, rows, cells)


def tile_row(row, x, columns):
    return (lax.div(row, SUB) * columns + x) * SUB + lax.rem(row, SUB)


def block_tile_row(block, columns):
    return tile_row(lax.div(block, columns), lax.rem(block, columns), columns)


def aligned(index, step):
    return pl.multiple_of(index * step, step)


def loop(count, body, unroll=1):
    def step(i, carry):
        body(i)
        return carry

    lax.fori_loop(0, count, step, 0, unroll=min(unroll, count))


class Copies:
    def __init__(self, semaphores):
        self.semaphores, self.open, self.used = semaphores, {}, 0

    def start(self, name, source, target):
        copy = pltpu.make_async_copy(source, target, self.semaphores.at[self.used])
        self.used += 1
        copy.start()
        self.open[name] = copy

    def wait(self, *names):
        for name in names:
            self.open.pop(name).wait()

    def wait_all(self):
        self.wait(*list(self.open))


def parts_of(count, parts):
    parts = parts if count % parts == 0 else 1
    return [pl.ds(i * (count // parts), count // parts) for i in range(parts)]


def pick_kernel(dims, src_in, state_in, sent_out, slab_a, slab_b, src, state, sent, sems):
    rows, columns, levels, tiles = dims
    copies = Copies(sems)
    level_stride = rows * columns
    copies.start("src", src_in, src)
    for i, part in enumerate(parts_of(NF * level_stride, 4)):
        copies.start(("top", i), state_in.at[part], state.at[part])
    deep = pl.ds(NF * level_stride, (levels - NF) * level_stride)
    copies.start("deep", state_in.at[deep], state.at[deep])
    comp, tile = lax.axis_index("comp"), lax.axis_index("tile")
    other = (1 - comp) * tiles

    def blank(t):
        sent[comp * tiles + t] = jnp.zeros((CAP * NF, BLK), BF16)

    loop(tiles, blank, unroll=16)

    def one_tile(t):
        for pair in range(CAP // 2):
            two = []
            for k in (2 * pair, 2 * pair + 1):
                start = block_tile_row(src[k, t], columns)
                two.append(state[pl.ds(start, NF, stride=level_stride), :])
            both = jnp.concatenate(two, axis=0).astype(BF16)
            sent[other + t, pl.ds(2 * NF * pair, 2 * NF), :] = both

    copies.wait("src", *[("top", i) for i in range(len(parts_of(NF * level_stride, 4)))])
    loop(tiles, one_tile, unroll=16)
    for name, half in (("sent", other), ("own", comp * tiles)):
        where = pl.ds(half, tiles)
        copies.start(name, sent.at[where], sent_out.at[where])
    even = lax.rem(tile, 2) == 0
    copies.wait("deep")
    for slab, first in (
        (slab_a, jnp.where(even, rows - NSUB, 0)),
        (slab_b, jnp.where(even, 0, rows - NSUB)),
    ):
        for i in range(NSUB):
            for x in range(columns):
                start = tile_row(first + i, x, columns)
                value = state[pl.ds(start, levels, stride=level_stride), :]
                slab[(i * columns + x) * levels : (i * columns + x + 1) * levels, :] = value.astype(BF16)
    copies.wait_all()


def row_of(ref, r, columns, levels):
    return [ref[pl.ds(aligned(r * columns + x, levels), levels), :] for x in range(columns)]


def rows_of_tile(ref, rt, x, columns, level_stride, levels):
    tall = []
    for half in range(levels // SUB):
        tiles = []
        for level in range(half * SUB, (half + 1) * SUB):
            start = pl.multiple_of(level * level_stride + (rt * columns + x) * SUB, SUB)
            tiles.append(ref[pl.ds(start, SUB), :])
        tall.append(jnp.transpose(jnp.stack(tiles), (1, 0, 2)))
    return [jnp.concatenate([t[i] for t in tall], axis=0) for i in range(SUB)]


def put_row(ref, r, values, columns, levels):
    for x, v in enumerate(values):
        ref[pl.ds(aligned(r * columns + x, levels), levels), :] = v


def stencil(rate, up, mid, down):
    columns = len(mid)
    keep = 1.0 - 4.0 * rate
    lane = lax.broadcasted_iota(jnp.int32, rate.shape, 1)
    right_roll = [pltpu.roll(v, 1, 1) for v in mid]
    left_roll = [pltpu.roll(v, BLK - 1, 1) for v in mid]
    out = []
    for x in range(columns):
        west = jnp.where(lane == 0, right_roll[x - 1], right_roll[x])
        east = jnp.where(lane == BLK - 1, left_roll[(x + 1) % columns], left_roll[x])
        out.append(keep * mid[x] + rate * (up[x] + down[x] + (west + east)))
    return out


def mixing_of(col_mix):
    mix_high = col_mix.astype(BF16)
    mix_low = (col_mix - mix_high.astype(F32)).astype(BF16)
    return jnp.concatenate([mix_high, mix_high, mix_low], axis=1)


def column_physics(diffused, mixing, land):
    whole = jnp.concatenate(diffused, axis=1)
    high = whole.astype(BF16)
    low = (whole - high.astype(F32)).astype(BF16)
    three = jnp.concatenate([high, low, high], axis=0)
    moved = whole + 0.5 * jnp.tanh(jnp.dot(mixing, three, preferred_element_type=F32))
    top = moved[:NF] - (0.5 * (1.0 - land)) * whole[:NF]
    columns = len(diffused)
    cut = lambda v: [v[:, x * BLK : (x + 1) * BLK] for x in range(columns)]
    return cut(top), cut(moved[NF:])


def inner_kernel(
    dims, kappa, state_in, mask_in, mix_in, weight_in, near, base_out, deep_out, mask_edge, mix, weight,
    mask, state, blocks, stepped, base, deep, sems,
):
    rows, columns, levels, _ = dims
    depth = levels - NF
    copies = Copies(sems)
    level_stride = rows * columns
    parts = parts_of(rows // SUB, 4)
    for i, part in enumerate(parts):
        where = pl.ds(part.start * columns * SUB, part.size * columns * SUB)
        copies.start(i, state_in.at[:, where], state.at[:, where])
    copies.start("mask", mask_in, mask)
    copies.start("mix", mix_in, mix)
    copies.start("weight", weight_in, weight)
    flat = state.reshape(levels * level_stride, BLK)
    rate = kappa[...]

    def one_tile_row(rt):
        for x in range(columns):
            for i, value in enumerate(rows_of_tile(flat, rt, x, columns, level_stride, levels)):
                where = (rt * SUB + i) * columns + x
                blocks[pl.ds(aligned(where, levels), levels), :] = value

    def first_step(r):
        around = [row_of(blocks, r + i, columns, levels) for i in (-1, 0, 1)]
        put_row(stepped, r, stencil(rate, *around), columns, levels)

    done = 1
    for i, part in enumerate(parts):
        copies.wait(i)
        first, size = part.start * SUB, part.size * SUB
        loop(part.size, lambda rt, part=part: one_tile_row(part.start + rt), unroll=part.size)
        last = first + size - 1
        loop(last - done, lambda r, done=done: first_step(done + r), unroll=last - done)
        done = last
    for i, r in enumerate((0, 1, rows - 2, rows - 1)):
        put_row(near, i, row_of(blocks, r, columns, levels), columns, levels)
    for i, r in enumerate((1, 2, rows - 3, rows - 2)):
        put_row(near, 4 + i, row_of(stepped, r, columns, levels), columns, levels)
    copies.wait("mask", "mix")
    for i, r in enumerate((0, 1, rows - 2, rows - 1)):
        mask_edge[i : i + 1, :] = mask[0, r : r + 1, :]
    mixing = mixing_of(mix[...])

    def second_step(i):
        r = i + 2
        around = [row_of(stepped, r + j, columns, levels) for j in (-1, 0, 1)]
        land = mask[0, pl.ds(r, 1), :].astype(F32)
        top, rest = column_physics(stencil(rate, *around), mixing, land)
        put_row(base, r, top, columns, NF)
        put_row(deep, r, rest, columns, depth)

    for first, last in ((0, rows - 20), (rows - 20, rows - 10), (rows - 10, rows - 4)):
        loop(last - first, lambda i, first=first: second_step(first + i), unroll=28)
        for name, source, target, size in (("base", base, base_out, NF), ("deep", deep, deep_out, depth)):
            middle = pl.ds((2 + first) * columns * size, (last - first) * columns * size)
            copies.start((name, first), source.at[middle], target.at[middle])
    copies.wait_all()


def edge_kernel(dims, kappa, near, mask_edge, mix, from_a, from_b, base_edge, deep, stepped, sems):
    _, columns, levels, tiles = dims
    tile = lax.axis_index("tile")
    even = lax.rem(tile, 2) == 0
    above_in = jnp.where(tile > 0, 1.0, 0.0).astype(F32)
    below_in = jnp.where(tile < tiles - 1, 1.0, 0.0).astype(F32)
    rate = kappa[...]
    mixing = mixing_of(mix[...])

    def slab_row(above, i):
        first, second = (from_b, from_a) if above else (from_a, from_b)
        return [
            jnp.where(even, p.astype(F32), q.astype(F32))
            for p, q in zip(
                row_of(first, i, columns, levels), row_of(second, i, columns, levels), strict=True
            )
        ]

    old = [row_of(near, i, columns, levels) for i in range(4)]
    above = [slab_row(True, i) for i in range(NSUB)]
    below = [slab_row(False, i) for i in range(NSUB)]
    new = [
        [v * above_in for v in stencil(rate, above[0], above[1], old[0])],
        stencil(rate, above[1], old[0], old[1]),
        stencil(rate, old[2], old[3], below[0]),
        [v * below_in for v in stencil(rate, old[3], below[0], below[1])],
    ]
    for i, values in enumerate(new):
        put_row(stepped, i, values, columns, levels)
    new = lambda i: row_of(stepped, i, columns, levels)
    at = lambda i: row_of(near, 4 + i, columns, levels)
    for i, around in enumerate(
        (
            (new(0), new(1), at(0)),
            (new(1), at(0), at(1)),
            (at(2), at(3), new(2)),
            (at(3), new(2), new(3)),
        )
    ):
        land = mask_edge[i : i + 1, :].astype(F32)
        top, rest = column_physics(stencil(rate, *around), mixing, land)
        put_row(base_edge, i, top, columns, NF)
        put_row(deep, i, rest, columns, levels - NF)


def surface_kernel(
    dims, arrived, base_edge, deep_edge, weight_in, dst_in, live_in_in, src_in, live_out_in, base_in, lagged_in, mask_in, weight_out_in,
    sent_out, top_out, flux_out, deep_edge_out,
    dst, live_in, src, live_out, base, lagged, mask, weight_out, sent, top, flux,
    numerator, denominator, sems,
):
    rows, columns, _, tiles = dims
    copies = Copies(sems)
    copies.start("dst", dst_in, dst)
    copies.start("live_in", live_in_in, live_in)
    tile_parts = parts_of(tiles, 4)
    middle = pl.ds(2 * columns * NF, (rows - 4) * columns * NF)
    copies.start("base", base_in.at[middle], base.at[middle])
    copies.start("lagged", lagged_in, lagged)
    copies.start("mask", mask_in, mask)
    copies.start("src", src_in, src)
    copies.start("live_out", live_out_in, live_out)
    for i, part in enumerate(tile_parts):
        copies.start(("weight_out", i), weight_out_in.at[part], weight_out.at[part])
    copies.start("deep_edge", deep_edge, deep_edge_out)
    comp = lax.axis_index("comp")
    other, own = (1 - comp) * tiles, comp * tiles

    def clear(r):
        for x in range(columns):
            where = pl.ds(aligned(r * columns + x, NF), NF)
            numerator[where, :] = jnp.zeros((NF, BLK), F32)
            denominator[where, :] = jnp.zeros((NF, BLK), F32)

    loop(rows, clear, unroll=32)
    ones = jnp.ones((NF, BLK), F32)

    def receive(t):
        got = arrived[other + t].astype(F32)
        for k in range(CAP):
            both = jnp.concatenate([got[k * NF : (k + 1) * NF], ones], axis=0).astype(BF16)
            product = jnp.dot(both, weight_in[t, k], preferred_element_type=F32)
            live = jnp.where(k < live_in[t], 1.0, 0.0).astype(F32)
            product = product * live
            where = pl.ds(aligned(dst[k, t], NF), NF)
            numerator[where, :] += product[:NF]
            denominator[where, :] += product[NF:]

    copies.wait("dst", "live_in")
    loop(tiles, receive, unroll=16)
    copies.wait("lagged")
    atmosphere = jnp.where(comp == 0, 1.0, 0.0).astype(F32)

    def earlier(rt):
        for x in range(columns):
            for i, value in enumerate(rows_of_tile(lagged, rt, x, columns, rows * columns, NF)):
                where = (rt * SUB + i) * columns + x
                top[pl.ds(aligned(where, NF), NF), :] = value * atmosphere

    loop(rows // SUB, earlier, unroll=4)
    copies.wait("base", "mask")

    def one_row(r, held=base, held_row=None):
        held_row = r if held_row is None else held_row
        land_row = mask[0, pl.ds(r, 1), :].astype(F32)
        for x in range(columns):
            where = pl.ds(aligned(r * columns + x, NF), NF)
            land = land_row[:, x * BLK : (x + 1) * BLK]
            received = numerator[where, :] / jnp.maximum(denominator[where, :], 1.0)
            incoming = top[where, :] + received
            state = held[pl.ds(aligned(held_row * columns + x, NF), NF), :] + land * incoming
            top[where, :] = state
            flux[where, :] = land * jnp.tanh(state - incoming)

    loop(rows - 4, lambda i: one_row(i + 2), unroll=28)
    for i, r in enumerate((0, 1, rows - 2, rows - 1)):
        one_row(r, base_edge, i)
    copies.start("top", top, top_out)
    copies.start("flux", flux, flux_out)

    rows_of = lax.broadcasted_iota(jnp.int32, (SUB, BLK), 0)

    def send(t):
        sums = jnp.zeros((SUB, BLK), F32)
        for pair in range(CAP // 2):
            two = []
            for k in (2 * pair, 2 * pair + 1):
                picked = flux[pl.ds(aligned(src[k, t], NF), NF), :]
                both = jnp.concatenate([picked, ones], axis=0).astype(BF16)
                product = jnp.dot(both, weight_out[t, k], preferred_element_type=F32)
                product = product * jnp.where(k < live_out[t], 1.0, 0.0).astype(F32)
                two.append(product[:NF])
                sums = jnp.where((rows_of == k) | (rows_of == k + CAP), product[NF:], sums)
            both = jnp.concatenate(two, axis=0).astype(BF16)
            sent[other + t, pl.ds(2 * NF * pair, 2 * NF), :] = both
        high = sums.astype(BF16).astype(F32)
        sums = jnp.where(rows_of < CAP, high, sums - high)
        sums = jnp.concatenate([sums, jnp.zeros((SUB, BLK), F32)], axis=0)
        sent[own + t, pl.ds(0, 2 * SUB), :] = sums.astype(BF16)
        sent[own + t, pl.ds(2 * SUB, 2 * SUB), :] = jnp.zeros((2 * SUB, BLK), BF16)

    copies.wait("src", "live_out")
    copies.wait(*[("weight_out", i) for i in range(len(tile_parts))])
    for i, part in enumerate(parts_of(tiles, 2)):
        loop(part.size, lambda t, part=part: send(part.start + t), unroll=16)
        for half in (other, own):
            where = pl.ds(half + part.start, part.size)
            copies.start(("sent", i, half is own), sent.at[where], sent_out.at[where])
    copies.wait_all()


def write_kernel(dims, top_in, deep_in, deep_edge_in, flux_in, new_state_out, land_flux, land_blocks, top, deep, flux, new_state, sems):
    rows, columns, levels, _ = dims
    copies = Copies(sems)
    copies.start("top", top_in, top)
    depth = levels - NF
    row, two = columns * depth, 2 * columns * depth
    for name, source, first, target, size in (
        ("deep", deep_in, two, two, (rows - 4) * row),
        ("above", deep_edge_in, 0, 0, two),
        ("below", deep_edge_in, two, (rows - 2) * row, two),
    ):
        copies.start(name, source.at[pl.ds(first, size)], deep.at[pl.ds(target, size)])
    copies.start("flux", flux_in, flux)
    comp = lax.axis_index("comp")
    on_land = jnp.where(comp == 1, 1.0, 0.0).astype(F32)
    cut = NF * rows * columns

    def from_blocks(source, target, count, first, scale=None):
        def one(rt):
            for x in range(columns):
                for level in range(count):
                    out = ((level + first) * (rows // SUB) + rt) * columns + x
                    start = (rt * SUB * columns + x) * count + level
                    value = source[pl.ds(start, SUB, stride=columns * count), :]
                    value = value if scale is None else value * scale
                    target[pl.ds(aligned(out, SUB), SUB), :] = value

        loop(rows // SUB, one, unroll=4)

    copies.wait("top")
    from_blocks(top, new_state, NF, 0)
    copies.start("state", new_state.at[pl.ds(0, cut)], new_state_out.at[pl.ds(0, cut)])
    copies.wait("deep", "above", "below")
    from_blocks(deep, new_state, depth, NF)
    rest = pl.ds(cut, depth * rows * columns)
    copies.start("rest", new_state.at[rest], new_state_out.at[rest])
    copies.wait("flux")
    from_blocks(flux, land_flux, NF, 0, on_land)
    land_blocks[...] = flux[...] * on_land
    copies.wait_all()


def return_kernel(dims, arrived, land_flux, land_blocks, dst_in, fluxes_out, dst, fluxes, numerator, denominator, sems):
    rows, columns, _, tiles = dims
    copies = Copies(sems)
    copies.start("dst", dst_in, dst)
    halves = parts_of(NF * rows * columns, 1)
    for i, part in enumerate(halves):
        copies.start(i, land_flux.at[part], fluxes.at[part])
    comp = lax.axis_index("comp")
    other = (1 - comp) * tiles
    level_stride = rows * columns

    def clear(r):
        for x in range(columns):
            where = pl.ds(aligned(r * columns + x, NF), NF)
            numerator[where, :] = jnp.zeros((NF, BLK), F32)
            denominator[where, :] = jnp.zeros((NF, BLK), F32)

    loop(rows, clear, unroll=32)

    def receive(t):
        got = arrived[other + t].astype(F32)
        sums = arrived[comp * tiles + t].astype(F32)
        sums = sums[:CAP] + sums[CAP : 2 * CAP]
        for k in range(CAP):
            where = pl.ds(aligned(dst[k, t], NF), NF)
            numerator[where, :] += got[k * NF : (k + 1) * NF]
            denominator[where, :] += jnp.broadcast_to(sums[k : k + 1], (NF, BLK))

    copies.wait("dst")
    loop(tiles, receive, unroll=16)
    copies.wait_all()

    def finish(t):
        for k in range(CAP):
            block = dst[k, t]
            where = pl.ds(aligned(block, NF), NF)
            out = pl.ds(block_tile_row(block, columns), NF, stride=level_stride)
            value = numerator[where, :] / jnp.maximum(denominator[where, :], 1.0)
            fluxes[out, :] = land_blocks[where, :] + value

    loop(tiles, finish, unroll=16)
    for i, part in enumerate(halves):
        copies.start(("out", i), fluxes.at[part], fluxes_out.at[part])
    copies.wait_all()


def call(kernel, operands, places, outs, scratch, copies, limit, cost):
    vmem, hbm = pl.BlockSpec(memory_space=pltpu.VMEM), pl.BlockSpec(memory_space=pltpu.HBM)
    spec = {"v": vmem, "m": vmem, "h": hbm}
    space = {"m": pltpu.VMEM, "h": pltpu.HBM}
    operands = [
        pltpu.with_memory_space_constraint(x, space[place]) if place in space else x
        for x, place in zip(operands, places, strict=True)
    ]
    return pl.pallas_call(
        kernel,
        out_shape=[out for out, _ in outs],
        in_specs=[spec[place] for place in places],
        out_specs=[spec[place] for _, place in outs],
        scratch_shapes=[*scratch, pltpu.SemaphoreType.DMA((copies,))],
        compiler_params=pltpu.CompilerParams(vmem_limit_bytes=limit),
        cost_estimate=pl.CostEstimate(flops=cost, bytes_accessed=cost // 4, transcendentals=0),
    )(*operands)


def per_device(
    state,
    kappa,
    col_mix,
    surface_mask,
    lagged_flux,
    a2l_src,
    a2l_dst,
    a2l_count,
    a2l_weight,
    l2a_src,
    l2a_dst,
    l2a_count,
    l2a_weight,
):
    fields = state[0]
    levels, rows, cells = fields.shape
    columns = cells // BLK
    nblocks = rows * columns
    tiles = lax.axis_size("tile")
    dims = (rows, columns, levels, tiles)
    shape, vmem, smem = pltpu.HBM, pltpu.VMEM, pltpu.SMEM
    kernel = lambda f: functools.partial(f, dims)
    limit = VMEM_LIMIT + 4 * tiles * CAP * BLK * BLK
    state_tiles = tile_view(fields)
    slab = (NSUB * columns * levels, BLK)
    parcel = (2 * tiles, CAP * NF, BLK)
    top_shape = (nblocks * NF, BLK)
    deep_shape = (nblocks * (levels - NF), BLK)
    full_shape = (nblocks * levels, BLK)
    weight_shape = (tiles, CAP, BLK, BLK)
    slots, counts = smem((CAP, tiles), jnp.int32), smem((tiles,), jnp.int32)
    sent, slab_a, slab_b = call(
        kernel(pick_kernel), [a2l_src[:, 0, :].T, state_tiles], "hh",
        [(shape(parcel, BF16), "h"), (vmem(slab, BF16), "v"), (vmem(slab, BF16), "v")],
        [slots, vmem(full_shape, F32), vmem(parcel, BF16)],
        8, limit, 4_000_000,
    )
    arrived = lax.all_to_all(sent, ("comp", "tile"), split_axis=0, concat_axis=0, tiled=True)
    from_a = lax.ppermute(slab_a, "tile", [(i, i ^ 1) for i in range(tiles)])
    pairs = [(i, i + 1) for i in range(1, tiles - 1, 2)]
    from_b = lax.ppermute(slab_b, "tile", pairs + [(j, i) for i, j in pairs])
    rates = jnp.broadcast_to(kappa[0][:, None], (levels, BLK))
    near, base, deep, mask_edge, mix, weight_in = call(
        kernel(inner_kernel),
        [rates, state_tiles.reshape(levels, nblocks, BLK), surface_mask, col_mix[0], a2l_weight[0]], "vhhhh",
        [(vmem((8 * columns * levels, BLK), F32), "v"), (shape(top_shape, F32), "h"),
         (shape(deep_shape, F32), "h"), (vmem((4, cells), jnp.int32), "v"),
         (vmem((levels, levels), F32), "v"), (vmem(weight_shape, BF16), "v")],
        [vmem((1, rows, cells), jnp.int32), vmem((levels, nblocks, BLK), F32), vmem(full_shape, F32),
         vmem(full_shape, F32), vmem(top_shape, F32), vmem(deep_shape, F32)],
        16, limit, 20_000_000,
    )
    base_edge, deep_near = call(
        kernel(edge_kernel), [rates, near, mask_edge, mix, from_a, from_b], "vvvvvv",
        [(vmem((4 * columns * NF, BLK), F32), "v"), (vmem((4 * columns * (levels - NF), BLK), F32), "v")],
        [vmem((4 * columns * levels, BLK), F32)],
        1, limit, 4_000_000,
    )
    sent_back, top, flux, deep_edge = call(
        kernel(surface_kernel),
        [arrived, base_edge, deep_near, weight_in, a2l_dst[0].T, a2l_count[0], l2a_src[:, 0, :].T,
         l2a_count[:, 0], base, tile_view(lagged_flux), surface_mask, l2a_weight[:, 0]], "vvvvhhhhhhhh",
        [(shape(parcel, BF16), "h"), (shape(top_shape, F32), "h"), (shape(top_shape, F32), "h"),
         (shape((4 * columns * (levels - NF), BLK), F32), "h")],
        [slots, counts, slots, counts, vmem(top_shape, F32), vmem(top_shape, F32), vmem((1, rows, cells), jnp.int32),
         vmem(weight_shape, BF16), vmem(parcel, BF16), vmem(top_shape, F32), vmem(top_shape, F32), vmem(top_shape, F32), vmem(top_shape, F32)],
        23, limit, 20_000_000,
    )
    returned = lax.all_to_all(
        sent_back, ("comp", "tile"), split_axis=0, concat_axis=0, tiled=True
    )
    new_state, land_flux, land_blocks = call(
        kernel(write_kernel), [top, deep, deep_edge, flux], "hhhh",
        [(shape(full_shape, F32), "h"), (vmem(top_shape, F32), "v"), (vmem(top_shape, F32), "v")],
        [vmem(top_shape, F32), vmem(deep_shape, F32), vmem(top_shape, F32), vmem(full_shape, F32),
         ],
        8, limit, 20_000_000,
    )
    (fluxes,) = call(
        kernel(return_kernel), [returned, land_flux, land_blocks, l2a_dst[0].T], "vvvm",
        [(shape(top_shape, F32), "h")],
        [slots, vmem(top_shape, F32), vmem(top_shape, F32), vmem(top_shape, F32)],
        6, limit, 10_000_000,
    )
    return (
        from_tile_view(new_state, levels, rows, cells)[None],
        from_tile_view(fluxes, NF, rows, cells)[None],
    )


def solution(mesh):
    return jax.shard_map(
        per_device,
        mesh=mesh,
        in_specs=(
            P("comp", None, "tile", None),
            P("comp", None),
            P("comp", None, None),
            P("comp", "tile", None),
            P(None, "tile", None),
            P(None, "tile", None),
            P("tile", None, None),
            P("tile", None),
            P("tile", None, None, None, None),
            P(None, "tile", None),
            P("tile", None, None),
            P(None, "tile"),
            P(None, "tile", None, None, None),
        ),
        out_specs=(P("comp", None, "tile", None), P("comp", None, "tile", None)),
        check_vma=False,
    )
```
